32 devices in a mesh: dp: 8 (over z, x), tensor: 4 (over y, core).
Axes of the slice: x: 2, y: 2, z: 4, core: 2. Of those that a mesh axis runs over, the one named last changes fastest.
Arguments:
- tokens: bfloat16 [8192, 1536], P(('dp', 'tensor')), may hold values from -6 to 6
- cotangent: bfloat16 [8192, 1536], P(('dp', 'tensor')), may hold values from -6 to 6
- prefix: int32 [8], P('dp'), may hold values from 0 to 1024
- routes: int32 [8192, 8], P('dp'), may hold values from 0 to 39, all different within a row; in each aligned block of 1024 rows (0 to 1023, 1024 to 2047, ...) at most 256 rows name the same one
- norm1: bfloat16 [1536], P('dp'), may hold values from 0.5 to 1.5
- w_query: bfloat16 [1536, 1536], P('dp', 'tensor'), may hold values from -0.15625 to 0.15625
- w_key: bfloat16 [1536, 512], P('dp', 'tensor'), may hold values from -0.15625 to 0.15625
- w_value: bfloat16 [1536, 512], P('dp', 'tensor'), may hold values from -0.15625 to 0.15625
- w_out: bfloat16 [1536, 1536], P('tensor', 'dp'), may hold values from -2.5 to 2.5
- norm2: bfloat16 [1536], P('dp'), may hold values from 0.5 to 1.5
- w_router: bfloat16 [1536, 40], P('dp'), may hold values from -0.076171875 to 0.076171875
- w_gate: bfloat16 [40, 1536, 512], P(None, 'dp', 'tensor'), may hold values from -0.15625 to 0.15625
- w_up: bfloat16 [40, 1536, 512], P(None, 'dp', 'tensor'), may hold values from -0.15625 to 0.15625
- w_down: bfloat16 [40, 512, 1536], P(None, 'tensor', 'dp'), may hold values from -1 to 1
Outputs:
- mixed: bfloat16 [8192, 1536], P(('dp', 'tensor'))
- grad_tokens: float32 [8192, 1536], P(('dp', 'tensor'))
- grad_norm1: float32 [1536], P('dp')
- grad_query: float32 [1536, 1536], P('dp', 'tensor')
- grad_key: float32 [1536, 512], P('dp', 'tensor')
- grad_value: float32 [1536, 512], P('dp', 'tensor')
- grad_out: float32 [1536, 1536], P('tensor', 'dp')
- grad_norm2: float32 [1536], P('dp')
- grad_router: float32 [1536, 40], P('dp')
- grad_gate: float32 [40, 1536, 512], P(None, 'dp', 'tensor')
- grad_up: float32 [40, 1536, 512], P(None, 'dp', 'tensor')
- grad_down: float32 [40, 512, 1536], P(None, 'tensor', 'dp')
The draws below stay inside these ranges and needn't reach their ends.
Inputs may be any that keep to these rules, and one draw needn't show every extreme that they name: `routes`: each row names 8 different experts. Among the 1024 rows of one index of dp no expert is named more than 256 times, and in every draw some expert is named exactly 256 times in some such block.
All inputs are finite; a program needn't handle non-finite values.
Results may differ from the reference program's by a relative error of at most 0.02.
Values may be sent and summed in bfloat16 or wider, within the bound.
No kernel may reach another device: no remote copies, remote signals or barrier semaphores. Data moves between devices by JAX's collectives and lax.ppermute only.
A program may use at most 448 MiB of HBM per device.

```python
import math
import jax
import jax.numpy as jnp
import numpy as np
from jax import lax

D = 1536
Q_HEADS = 24
KV_HEADS = 8
HEAD_DIM = 64
EXPERTS = 40
FF = 512
TOPK = 8
SEQ_LEN = 1024
GROUP = 1024
SEQS = 8
TOKENS = 8192
CAP = 256
N_DP = 8


def place_ends(array, stream_key, least, top_value):
    longest = array.shape.index(max(array.shape))
    spots = []
    for shift in (0, 1):
        where = [jax.random.randint(jax.random.fold_in(stream_key, axis), (), 0, length) for axis, length in enumerate(array.shape)]
        where[longest] = (where[longest] + shift) % array.shape[longest]
        spots.append(tuple(where))
    return array.at[spots[0]].set(least).at[spots[1]].set(top_value)


def shard_levels(stream_key, dims, cuts, smallest, high):
    level, own = 1.0, jax.random.fold_in(stream_key, 6)
    for axis_at, blocks in cuts:
        heights = jnp.exp(jax.random.uniform(jax.random.fold_in(own, axis_at), (blocks,), jnp.float32, smallest / len(cuts), high / len(cuts)))
        level = level * jnp.repeat(heights, dims[axis_at] // blocks).reshape([-1 if axis == axis_at else 1 for axis in range(len(dims))])
    return level


def routed_block(stream_key, own, number, rows, number_of, top, most, skew):
    sequence = jax.random.permutation(stream_key, number_of)
    heavy_load, usual = shares(number_of, rows * top, most, skew, True), shares(number_of, rows * top, most, skew, False)
    places = jnp.arange(number_of)

    def named(tallies, rotation):
        used = int((tallies > 0).sum())
        fixed = max(1, used // 4)
        moved = fixed + (places - fixed + rotation * (used - fixed)) % max(1, number_of - fixed)
        return jnp.zeros((number_of,), jnp.int32).at[sequence[jnp.where(places < fixed, places, moved)]].set(jnp.asarray(tallies, jnp.int32))

    tallies = jnp.where(number % 4 == 0, named(heavy_load, number // 4), named(usual, number - number // 4 - 1))
    mixed = jax.random.permutation(jax.random.fold_in(own, 3), number_of)
    giver, sink = mixed[0:number_of // 2 * 2:2], mixed[1:number_of // 2 * 2:2]
    room = jnp.minimum(tallies[giver] - 1, most - tallies[sink]) // 2
    room = jnp.where((giver == sequence[0]) | (sink == sequence[0]) | (tallies[sink] == 0), 0, jnp.maximum(room, 0))
    moved = jax.random.randint(jax.random.fold_in(own, 4), (number_of // 2,), 0, 1 << 20) % (room + 1)
    tallies = tallies.at[giver].add(-moved).at[sink].add(moved)
    items = jnp.searchsorted(jnp.cumsum(tallies), jnp.arange(rows * top), side="right").astype(jnp.int32)
    table = items.reshape(top, rows).T
    table = table[jax.random.permutation(jax.random.fold_in(own, 1), rows)]
    rotation = jax.random.randint(jax.random.fold_in(own, 2), (rows, 1), 0, top)
    return jnp.take_along_axis(table, (jnp.arange(top)[None, :] + rotation) % top, axis=1)


def shares(count, total, bound, skew, full):
    weights = [(1 << 20) // math.isqrt(rank ** skew) + 1 for rank in range(1, count + 1)]
    largest = bound if full else min(bound, max(-(-total // count), total * weights[0] // sum(weights)))
    least = 1 if total - largest >= count - 1 else 0
    holding, surplus = [largest] + [least] * (count - 1), total - largest - least * (count - 1)
    while surplus > 0:
        movable = [i for i in range(1, count) if holding[i] < largest] or [i for i in range(1, count) if holding[i] < bound]
        pool, remaining = sum([weights[i] for i in movable]), surplus
        for i in movable:
            more = min(bound - holding[i], max(1, remaining * weights[i] // pool), surplus)
            holding[i] = holding[i] + more
            surplus = surplus - more
    return np.array(holding)


def noise(stream_key, dims, scale, bound, pieces=(), kind=jnp.bfloat16):
    values = scale * jax.random.normal(stream_key, dims, jnp.float32)
    if pieces:
        values = values * shard_levels(stream_key, dims, pieces, -0.22, 0.18)
    return jnp.clip(values, -bound, bound).astype(kind)


def setup_inputs(seed: int = 0) -> dict:
    seeds = jax.random.split(jax.random.key(seed), 15)
    tokens = noise(seeds[0], (TOKENS, D), 1.0, 6.0, ((0, 32),))
    cotangent = noise(seeds[1], (TOKENS, D), 1.0, 6.0, ((0, 32),))
    prefix = place_ends(jax.random.randint(seeds[2], (SEQS,), 0, SEQ_LEN + 1), jax.random.fold_in(seeds[2], 1), 0, SEQ_LEN).astype(jnp.int32)
    routes_keys = jax.random.split(jax.random.fold_in(seeds[3], 1), TOKENS // GROUP)
    routes_turns = jax.random.permutation(jax.random.fold_in(seeds[3], 3), TOKENS // GROUP)
    routes = jax.vmap(lambda own, number: routed_block(jax.random.fold_in(seeds[3], 2), own, number, GROUP, EXPERTS, TOPK, CAP, 1))(routes_keys, routes_turns).reshape((TOKENS, TOPK))
    norm1 = jnp.clip(1.0 + 0.1 * jax.random.normal(seeds[4], (D,), jnp.float32), 0.5, 1.5).astype(jnp.bfloat16)
    w_query = noise(seeds[5], (D, Q_HEADS * HEAD_DIM), D ** -0.5, 0.15625, ((0, 8), (1, 4)))
    w_key = noise(seeds[6], (D, KV_HEADS * HEAD_DIM), D ** -0.5, 0.15625, ((0, 8), (1, 4)))
    w_value = noise(seeds[7], (D, KV_HEADS * HEAD_DIM), D ** -0.5, 0.15625, ((0, 8), (1, 4)))
    w_out = noise(seeds[8], (Q_HEADS * HEAD_DIM, D), (max(Q_HEADS * HEAD_DIM // 256, 1)) ** -0.5, 2.5, ((0, 4), (1, 8)))
    norm2 = jnp.clip(1.0 + 0.1 * jax.random.normal(seeds[9], (D,), jnp.float32), 0.5, 1.5).astype(jnp.bfloat16)
    w_router = noise(seeds[10], (D, EXPERTS), (0.5 / D ** 0.5), 0.076171875, ((0, 8),))
    w_gate = noise(seeds[11], (EXPERTS, D, FF), D ** -0.5, 0.15625, ((1, 8), (2, 4)))
    w_up = noise(seeds[12], (EXPERTS, D, FF), D ** -0.5, 0.15625, ((1, 8), (2, 4)))
    w_down = noise(seeds[13], (EXPERTS, FF, D), (max(FF // 16, 1)) ** -0.5, 1.0, ((1, 4), (2, 8)))
    return {"tokens": tokens, "cotangent": cotangent, "prefix": prefix, "routes": routes, "norm1": norm1, "w_query": w_query, "w_key": w_key, "w_value": w_value, "w_out": w_out, "norm2": norm2, "w_router": w_router, "w_gate": w_gate, "w_up": w_up, "w_down": w_down}


EPSILON = 1e-05
HIGHEST = lax.Precision.HIGHEST

@jax.custom_vjp
def low(v):
    return lax.optimization_barrier(v.astype(jnp.bfloat16)).astype(jnp.float32)

@jax.custom_vjp
def low_back(v):
    return v

def low_keep(v):
    return (low(v), None)

def low_pass(kept, grad):
    return (grad,)

def back_keep(v):
    return (v, None)

def back_low(kept, grad):
    return (low(grad),)
low.defvjp(low_keep, low_pass)
low_back.defvjp(back_keep, back_low)

def matmul(left, right):
    return jnp.dot(left, right, precision=HIGHEST)

def rms_norm(values, gain):
    return values * lax.rsqrt(lax.optimization_barrier(jnp.mean(values * values, axis=-1, keepdims=True)) + EPSILON) * gain

def rotate(tensor):
    half = HEAD_DIM // 2
    position = jnp.arange(SEQ_LEN, dtype=jnp.int32).astype(jnp.float32)
    inverse = jnp.power(10000.0, -jnp.arange(half, dtype=jnp.int32).astype(jnp.float32) / half)
    angle = position[:, None] * inverse[None, :]
    cosine = jnp.cos(angle)[:, None, :]
    sine = jnp.sin(angle)[:, None, :]
    first = tensor[..., :half]
    second = tensor[..., half:]
    return jnp.concatenate([first * cosine - second * sine, second * cosine + first * sine], axis=-1)

def attend_sequence(members):
    query, keys, values, prefix_len = members
    groups = Q_HEADS // KV_HEADS
    grouped = query.reshape(SEQ_LEN, KV_HEADS, groups, HEAD_DIM)
    scores = jnp.einsum('qhgd,khd->hgqk', grouped, keys, precision=HIGHEST) * HEAD_DIM ** (-0.5)
    scores = low_back(scores)
    row_ids = jnp.arange(SEQ_LEN, dtype=jnp.int32)
    allowed = (row_ids[None, :] <= row_ids[:, None]) | (row_ids[None, :] < prefix_len)
    scores = jnp.where(allowed, scores, -1e+30)
    weights = low(jax.nn.softmax(scores, axis=-1))
    output = jnp.einsum('hgqk,khd->qhgd', weights, values, precision=HIGHEST)
    return output.reshape(SEQ_LEN, Q_HEADS * HEAD_DIM)

def slot_index(group_routes):
    flat_experts = group_routes.reshape(-1)
    hits = (flat_experts[:, None] == jnp.arange(EXPERTS, dtype=jnp.int32)[None, :]).astype(jnp.int32)
    earlier = jnp.cumsum(hits, axis=0) - hits
    return (flat_experts * CAP + lax.optimization_barrier(jnp.sum(earlier * hits, axis=1))).astype(jnp.int32)

def slot_tokens(flat_slots):
    owners = jnp.arange(flat_slots.shape[0], dtype=jnp.int32) // TOPK
    return jnp.zeros((EXPERTS * CAP,), jnp.int32).at[flat_slots].set(owners)

def expert_group(members, gate_weights, up_weights, down_weights):
    normed, gates, flat_slots, owners = members
    stacked = normed[owners].reshape(EXPERTS, CAP, D)
    gate_part = low_back(jnp.einsum('ecd,edf->ecf', stacked, gate_weights, precision=HIGHEST))
    up_part = low_back(jnp.einsum('ecd,edf->ecf', stacked, up_weights, precision=HIGHEST))
    hidden = low(jax.nn.silu(gate_part) * up_part)
    expert_out = low_back(jnp.einsum('ecf,efd->ecd', hidden, down_weights, precision=HIGHEST))
    picked = expert_out.reshape(EXPERTS * CAP, D)[flat_slots].reshape(GROUP, TOPK, D)
    return jnp.einsum('tk,tkd->td', gates, picked, precision=HIGHEST)

def reference(tokens, cotangent, prefix, routes, norm1, w_query, w_key, w_value, w_out, norm2, w_router, w_gate, w_up, w_down):
    flat_slots = jax.vmap(slot_index)(routes.reshape(N_DP, GROUP, TOPK))
    owners = jax.vmap(slot_tokens)(flat_slots)

    def forward(values, gain_one, query_w, key_w, value_w, out_w, gain_two, router_w, gate_w, up_w, down_w):
        normed_one = low(rms_norm(values, gain_one))
        query = low_back(matmul(normed_one, query_w)).reshape(SEQS, SEQ_LEN, Q_HEADS, HEAD_DIM)
        keys = low_back(matmul(normed_one, key_w)).reshape(SEQS, SEQ_LEN, KV_HEADS, HEAD_DIM)
        vals = low(low_back(matmul(normed_one, value_w))).reshape(SEQS, SEQ_LEN, KV_HEADS, HEAD_DIM)
        query = low(jax.vmap(rotate)(query))
        keys = low(jax.vmap(rotate)(keys))
        attended = lax.map(jax.checkpoint(attend_sequence), (query, keys, vals, prefix))
        attended = low(low_back(attended.reshape(TOKENS, Q_HEADS * HEAD_DIM)))
        middle = values + low_back(matmul(attended, out_w))
        normed_two = low(rms_norm(middle, gain_two))
        logits = matmul(normed_two, router_w)
        chosen = jnp.take_along_axis(logits, routes, axis=1)
        gates = jax.nn.softmax(chosen, axis=-1)

        def one_group(members):
            return expert_group(members, gate_w, up_w, down_w)
        expert_sum = lax.map(jax.checkpoint(one_group), (normed_two.reshape(N_DP, GROUP, D), gates.reshape(N_DP, GROUP, TOPK), flat_slots, owners))
        return middle + expert_sum.reshape(TOKENS, D)
    params = (tokens.astype(jnp.float32), norm1.astype(jnp.float32), w_query.astype(jnp.float32), w_key.astype(jnp.float32), w_value.astype(jnp.float32), w_out.astype(jnp.float32), norm2.astype(jnp.float32), w_router.astype(jnp.float32), w_gate.astype(jnp.float32), w_up.astype(jnp.float32), w_down.astype(jnp.float32))
    output, pullback = jax.vjp(forward, *params)
    grads = pullback(cotangent.astype(jnp.float32))
    return (output.astype(jnp.bfloat16), grads[0], grads[1], grads[2], grads[3], grads[4], grads[5], grads[6], grads[7], grads[8], grads[9], grads[10])
```

```python
import jax
import jax.numpy as jnp
from jax import lax
from jax.sharding import Mesh, PartitionSpec as P

HEAD_DIM = 64
EPSILON = 1e-05
LANES = 128
HIGHEST = lax.Precision.HIGHEST
f32 = jnp.float32
bf16 = jnp.bfloat16


def rms_scale(values):
    return lax.rsqrt(jnp.mean(values * values, axis=-1, keepdims=True) + EPSILON)


def norm_backward(values, scale, gain, grad_normed):
    normal_x = values * scale
    grad_hat = grad_normed * gain
    grad_values = scale * (
        grad_hat - normal_x * jnp.mean(grad_hat * normal_x, axis=-1, keepdims=True)
    )
    return grad_values, normal_x


def rotary_tables(row_count, half):
    position = jnp.arange(row_count, dtype=jnp.int32).astype(f32)
    inverse = jnp.power(10000.0, -jnp.arange(half, dtype=jnp.int32).astype(f32) / half)
    angle = position[:, None] * inverse[None, :]
    return jnp.cos(angle)[:, None, :], jnp.sin(angle)[:, None, :]


def rotate(tensor, cosine, sine):
    half = tensor.shape[-1] // 2
    first = tensor[..., :half]
    second = tensor[..., half:]
    return jnp.concatenate(
        [first * cosine - second * sine, second * cosine + first * sine], axis=-1
    )


def masked_scores(query, keys, prefix_len):
    seq_len, heads_kv, head_size = keys.shape
    grouped = query.reshape(seq_len, heads_kv, -1, head_size)
    scores = jnp.einsum(
        "qhgd,khd->hgqk", grouped, keys, preferred_element_type=f32
    ) * head_size ** (-0.5)
    row_ids = jnp.arange(seq_len, dtype=jnp.int32)
    allowed = (row_ids[None, :] <= row_ids[:, None]) | (row_ids[None, :] < prefix_len)
    return jnp.where(allowed, scores, -1e30), grouped


def attend_forward(query, keys, values, prefix_len):
    scores, _ = masked_scores(query, keys, prefix_len)
    highest = jnp.max(scores, axis=-1, keepdims=True)
    shifted = jnp.exp(scores - highest)
    summed = jnp.sum(shifted, axis=-1, keepdims=True)
    weights = (shifted / summed).astype(bf16)
    output = jnp.einsum("hgqk,khd->qhgd", weights, values, preferred_element_type=f32)
    return output.reshape(query.shape[0], -1).astype(bf16), highest + jnp.log(summed)


def attend_backward(query, keys, values, grad_mixed, log_total, prefix_len):
    scores, grouped = masked_scores(query, keys, prefix_len)
    weights = jnp.exp(scores - log_total)
    seq_len, heads_kv, head_size = keys.shape
    grad_grouped = grad_mixed.reshape(seq_len, heads_kv, -1, head_size)
    grad_weights = jnp.einsum(
        "qhgd,khd->hgqk", grad_grouped, values, preferred_element_type=f32
    )
    grad_scores = (
        weights * (grad_weights - jnp.sum(weights * grad_weights, axis=-1, keepdims=True))
    ).astype(bf16)
    scaling = head_size ** (-0.5)
    grad_query = (
        jnp.einsum("hgqk,khd->qhgd", grad_scores, keys, preferred_element_type=f32) * scaling
    )
    grad_keys = (
        jnp.einsum("hgqk,qhgd->khd", grad_scores, grouped, preferred_element_type=f32) * scaling
    )
    grad_values = jnp.einsum(
        "hgqk,qhgd->khd", weights.astype(bf16), grad_grouped, preferred_element_type=f32
    )
    return grad_query.reshape(seq_len, -1, head_size), grad_keys, grad_values


def exchange(pieces, axis, size):
    me = lax.axis_index(axis)
    result = jnp.zeros_like(pieces)
    own = lax.dynamic_index_in_dim(pieces, me, 0)
    result = lax.dynamic_update_slice_in_dim(result, own, me, 0)
    for shift in range(1, size):
        piece = lax.dynamic_index_in_dim(pieces, (me + shift) % size, 0)
        got = lax.ppermute(piece, axis, [(m, (m + shift) % size) for m in range(size)])
        result = lax.dynamic_update_slice_in_dim(result, got, (me - shift) % size, 0)
    return result


def solution(mesh):
    n_dp, n_tensor = mesh.shape["dp"], mesh.shape["tensor"]
    inner = 4
    outer = n_dp // inner
    grid = Mesh(mesh.devices.reshape(inner, outer, n_tensor), ("i", "o", "t"))
    dp = ("i", "o")
    shared = ("i", "t")

    def to_owner_order(values):
        rows = values.shape[0]
        if outer == 1:
            return values
        split = jnp.swapaxes(values.reshape(rows, inner, outer, -1), 1, 2)
        if outer == 2:
            split = jnp.where(lax.axis_index("o") == 0, split, split[:, ::-1])
        return split.reshape(rows, -1)

    def from_owner_order(values):
        rows = values.shape[0]
        if outer == 1:
            return values
        split = values.reshape(rows, outer, inner, -1)
        if outer == 2:
            split = jnp.where(lax.axis_index("o") == 0, split, split[:, ::-1])
        return jnp.swapaxes(split, 1, 2).reshape(rows, -1)

    def gather_outer(values):
        if outer == 1:
            return values
        if outer == 2:
            other = lax.ppermute(values, "o", [(0, 1), (1, 0)])
            return jnp.concatenate([values, other], axis=0)
        return lax.all_gather(values, "o", axis=0, tiled=True)

    def reduce_outer(values):
        if outer == 1:
            return values.astype(bf16)
        if outer == 2:
            rows = values.shape[0] // 2
            got = lax.ppermute(values[rows:].astype(bf16), "o", [(0, 1), (1, 0)])
            return (values[:rows] + got.astype(f32)).astype(bf16)
        return lax.psum_scatter(values.astype(bf16), "o", scatter_dimension=0, tiled=True)

    def on_device(
        tokens,
        cotangent,
        prefix,
        routes,
        norm1,
        w_query,
        w_key,
        w_value,
        w_out,
        norm2,
        w_router,
        w_gate,
        w_up,
        w_down,
    ):
        rows, width = tokens.shape
        group = routes.shape[0]
        n_experts, depth, hidden = w_gate.shape
        own_experts = n_experts // inner
        own_hidden = own_experts * hidden
        q_cols, k_cols = w_query.shape[1], w_key.shape[1]
        qkv_cols = q_cols + 2 * k_cols
        attn_cols = qkv_cols + q_cols
        side_cols = -(-(n_experts + 2) // LANES) * LANES
        gate_cols = -(-2 * n_experts // LANES) * LANES
        me_i, me_t = lax.axis_index("i"), lax.axis_index("t")

        weights3 = jnp.stack([w_gate, w_up, jnp.swapaxes(w_down, 1, 2)])
        pieces = weights3.reshape(3, inner, own_experts, depth, hidden)
        pieces = pieces.transpose(1, 3, 0, 2, 4).reshape(inner, depth, 3 * own_hidden)
        owned = gather_outer(exchange(pieces, "i", inner).reshape(inner * depth, -1))
        w_gate_up = owned[:, : 2 * own_hidden]
        w_down_t = owned[:, 2 * own_hidden :]

        side = jnp.concatenate(
            [
                w_router,
                norm1[:, None],
                norm2[:, None],
                jnp.zeros((depth, side_cols - n_experts - 2), bf16),
            ],
            axis=1,
        )
        pack = jnp.concatenate([w_query, w_key, w_value, w_out.T, side], axis=1)
        packed = lax.all_gather(pack, dp, axis=0, tiled=True)
        tokens_all = lax.all_gather(tokens, "t", axis=0, tiled=True).astype(f32)
        w_qkv = packed[:, :qkv_cols]
        w_out_t = packed[:, qkv_cols:attn_cols]
        router = packed[:, attn_cols : attn_cols + n_experts]
        gains = packed[:, attn_cols + n_experts : attn_cols + n_experts + 2].astype(f32).T
        gain_one, gain_two = gains[0], gains[1]

        cot_order, _ = lax.optimization_barrier((to_owner_order(cotangent), tokens_all))
        cot_all = lax.all_gather(cot_order, shared, axis=0, tiled=True)

        normal_all = tokens_all * rms_scale(tokens_all)
        normed_one = (normal_all * gain_one).astype(bf16)
        cosine, sine = rotary_tables(group, HEAD_DIM // 2)
        qkv = jnp.dot(normed_one, w_qkv, preferred_element_type=f32)
        query = rotate(qkv[:, :q_cols].reshape(group, -1, HEAD_DIM), cosine, sine).astype(bf16)
        keys = rotate(
            qkv[:, q_cols : q_cols + k_cols].reshape(group, -1, HEAD_DIM), cosine, sine
        ).astype(bf16)
        values = qkv[:, q_cols + k_cols :].astype(bf16).reshape(group, -1, HEAD_DIM)
        attended, log_total = attend_forward(query, keys, values, prefix[0])
        branch = lax.dot_general(
            attended, w_out_t, (((1,), (1,)), ((), ())), preferred_element_type=f32
        ).astype(bf16)
        tokens_f = tokens.astype(f32)
        middle = tokens_f + lax.psum_scatter(
            branch, "t", scatter_dimension=0, tiled=True
        ).astype(f32)
        scale_two = rms_scale(middle)
        normed_two = (middle * scale_two * gain_two).astype(bf16)

        logits = jnp.dot(normed_two, router, preferred_element_type=f32)
        own_routes = lax.dynamic_slice_in_dim(routes, me_t * rows, rows, 0)
        expert_ids = jnp.arange(n_experts, dtype=jnp.int32)
        routed = jnp.any(own_routes[:, :, None] == expert_ids[None, None, :], axis=1)
        gates = jnp.where(routed, jax.nn.softmax(jnp.where(routed, logits, -1e30), axis=-1), 0.0)
        gates_high = gates.astype(bf16)
        gates_low = (gates - gates_high.astype(f32)).astype(bf16)
        shipped = jnp.concatenate(
            [
                to_owner_order(normed_two),
                gates_high,
                gates_low,
                jnp.zeros((rows, gate_cols - 2 * n_experts), bf16),
            ],
            axis=1,
        )
        shared_all = lax.all_gather(shipped, shared, axis=0, tiled=True)
        count = shared_all.shape[0]
        normed_all = shared_all[:, :width]

        slot = jnp.arange(gate_cols, dtype=jnp.int32)[:, None]
        owner = me_i * own_experts + jnp.arange(own_hidden, dtype=jnp.int32)[None, :] // hidden
        spread = ((slot == owner) | (slot == owner + n_experts)).astype(bf16)
        gate_wide = jnp.dot(shared_all[:, width:], spread, preferred_element_type=f32)
        gate_up = jnp.dot(normed_all, w_gate_up, preferred_element_type=f32)
        gate_part, up_part = gate_up[:, :own_hidden], gate_up[:, own_hidden:]
        cot_part = jnp.dot(cot_all, w_down_t, preferred_element_type=f32)
        sigmoid_g = jax.nn.sigmoid(gate_part)
        silu_g = gate_part * sigmoid_g
        act = silu_g * up_part
        gated = (act * gate_wide).astype(bf16)
        grad_act = cot_part * gate_wide
        grad_gate_up = jnp.concatenate(
            [
                (grad_act * up_part * sigmoid_g * (1.0 + gate_part * (1.0 - sigmoid_g))).astype(
                    bf16
                ),
                (grad_act * silu_g).astype(bf16),
            ],
            axis=1,
        )
        grad_gates = jnp.sum((act * cot_part).reshape(count, own_experts, hidden), axis=-1)
        gate_block = lax.dynamic_update_slice(
            jnp.zeros((count, side_cols), f32), grad_gates, (0, me_i * own_experts)
        )
        grad_normed_part = lax.dot_general(
            grad_gate_up, w_gate_up, (((1,), (1,)), ((), ())), preferred_element_type=f32
        )
        grad_shipped = jnp.concatenate([grad_normed_part, gate_block], axis=1).astype(bf16)
        grad_back = lax.psum_scatter(grad_shipped, shared, scatter_dimension=0, tiled=True)

        expert_part = lax.dot_general(
            gated, w_down_t, (((1,), (1,)), ((), ())), preferred_element_type=f32
        ).astype(bf16)
        contract_rows = (((0,), (0,)), ((), ()))
        grad_w = jnp.concatenate(
            [
                lax.dot_general(
                    normed_all, grad_gate_up, contract_rows, preferred_element_type=f32
                ),
                lax.dot_general(cot_all, gated, contract_rows, preferred_element_type=f32),
            ],
            axis=1,
        )

        grad_back = grad_back.astype(f32)
        grad_chosen = grad_back[:, width : width + n_experts]
        grad_logits = gates * (
            grad_chosen - jnp.sum(gates * grad_chosen, axis=-1, keepdims=True)
        )
        grad_normed_two = from_owner_order(grad_back[:, :width]) + jnp.dot(
            grad_logits, router.astype(f32).T, precision=HIGHEST
        )
        grad_middle_part, normal_two = norm_backward(
            middle, scale_two, gain_two, grad_normed_two
        )
        grad_middle = cotangent.astype(f32) + grad_middle_part
        grad_gain_two = jnp.sum(grad_normed_two * normal_two, axis=0)
        grad_router_part = lax.dot_general(
            normed_two.astype(f32), grad_logits, contract_rows, precision=HIGHEST
        )
        grad_branch = lax.all_gather(grad_middle.astype(bf16), "t", axis=0, tiled=True)

        grad_branch_tie, expert_part = lax.optimization_barrier((grad_branch, expert_part))
        expert_share = from_owner_order(
            lax.psum_scatter(expert_part, shared, scatter_dimension=0, tiled=True)
        ).astype(f32)
        mixed = (middle + expert_share).astype(bf16)

        grad_attended = jnp.dot(
            grad_branch_tie, w_out_t, preferred_element_type=f32
        ).astype(bf16)
        grad_query, grad_keys, grad_values = attend_backward(
            query, keys, values, grad_attended, log_total, prefix[0]
        )
        grad_qkv = jnp.concatenate(
            [
                rotate(grad_query, cosine, -sine).astype(bf16).reshape(group, -1),
                rotate(grad_keys, cosine, -sine).astype(bf16).reshape(group, -1),
                grad_values.astype(bf16).reshape(group, -1),
            ],
            axis=1,
        )
        grad_normed_one = lax.dot_general(
            grad_qkv, w_qkv, (((1,), (1,)), ((), ())), preferred_element_type=f32
        )
        grad_gain_one = jnp.sum(grad_normed_one * normal_all, axis=0)
        own_grad_one = lax.psum_scatter(
            grad_normed_one.astype(bf16), "t", scatter_dimension=0, tiled=True
        ).astype(f32)
        grad_input_part, _ = norm_backward(tokens_f, rms_scale(tokens_f), gain_one, own_grad_one)
        grad_tokens = grad_middle + grad_input_part

        grad_attn = jnp.concatenate(
            [
                lax.dot_general(normed_one, grad_qkv, contract_rows, preferred_element_type=f32),
                lax.dot_general(grad_branch_tie, attended, contract_rows, preferred_element_type=f32),
            ],
            axis=1,
        ).astype(bf16)
        shard_attn = lax.psum_scatter(grad_attn, dp, scatter_dimension=0, tiled=True).astype(f32)
        sums = jnp.concatenate(
            [grad_router_part, grad_gain_one[:, None], grad_gain_two[:, None]], axis=1
        )
        sums = lax.psum(sums, ("i", "o", "t"))
        first = (me_i * outer + lax.axis_index("o")) * depth
        own_sums = lax.dynamic_slice_in_dim(sums, first, depth, 0)

        reduced = reduce_outer(grad_w).reshape(inner, depth, 3 * own_hidden)
        returned = exchange(reduced, "i", inner).reshape(inner, depth, 3, own_experts, hidden)
        grad3 = returned.transpose(2, 0, 3, 1, 4).reshape(3, n_experts, depth, hidden).astype(f32)
        return (
            mixed,
            grad_tokens,
            own_sums[:, n_experts],
            shard_attn[:, :q_cols],
            shard_attn[:, q_cols : q_cols + k_cols],
            shard_attn[:, q_cols + k_cols : qkv_cols],
            shard_attn[:, qkv_cols:].T,
            own_sums[:, n_experts + 1],
            own_sums[:, :n_experts],
            grad3[0],
            grad3[1],
            jnp.swapaxes(grad3[2], 1, 2),
        )

    in_specs = (
        P(("i", "o", "t"), None),
        P(("i", "o", "t"), None),
        P(dp),
        P(dp, None),
        P(dp),
        P(dp, "t"),
        P(dp, "t"),
        P(dp, "t"),
        P("t", dp),
        P(dp),
        P(dp, None),
        P(None, dp, "t"),
        P(None, dp, "t"),
        P(None, "t", dp),
    )
    out_specs = (
        P(("i", "o", "t"), None),
        P(("i", "o", "t"), None),
        P(dp),
        P(dp, "t"),
        P(dp, "t"),
        P(dp, "t"),
        P("t", dp),
        P(dp),
        P(dp, None),
        P(None, dp, "t"),
        P(None, dp, "t"),
        P(None, "t", dp),
    )
    return jax.shard_map(
        on_device, mesh=grid, in_specs=in_specs, out_specs=out_specs, check_vma=False
    )
```

```python
import jax
import jax.numpy as jnp
from jax import lax
from jax.experimental.layout import Layout, with_layout_constraint
from jax.sharding import Mesh, PartitionSpec as P

HEAD_DIM = 64
EPSILON = 1e-05
LANES = 128
HIGHEST = lax.Precision.HIGHEST
f32 = jnp.float32
bf16 = jnp.bfloat16


def rms_scale(values):
    return lax.rsqrt(jnp.mean(values * values, axis=-1, keepdims=True) + EPSILON)


def norm_backward(values, scale, gain, grad_normed):
    normal_x = values * scale
    grad_hat = grad_normed * gain
    grad_values = scale * (
        grad_hat - normal_x * jnp.mean(grad_hat * normal_x, axis=-1, keepdims=True)
    )
    return grad_values, normal_x


def rotary_tables(row_count, half):
    position = jnp.arange(row_count, dtype=jnp.int32).astype(f32)
    inverse = jnp.power(10000.0, -jnp.arange(half, dtype=jnp.int32).astype(f32) / half)
    angle = position[:, None] * inverse[None, :]
    return jnp.cos(angle)[:, None, :], jnp.sin(angle)[:, None, :]


def rotate(tensor, cosine, sine):
    half = tensor.shape[-1] // 2
    first = tensor[..., :half]
    second = tensor[..., half:]
    return jnp.concatenate(
        [first * cosine - second * sine, second * cosine + first * sine], axis=-1
    )


def masked_scores(query, keys, prefix_len):
    seq_len, heads_kv, head_size = keys.shape
    grouped = query.reshape(seq_len, heads_kv, -1, head_size)
    scores = jnp.einsum(
        "qhgd,khd->hgqk", grouped, keys, preferred_element_type=f32
    ) * head_size ** (-0.5)
    row_ids = jnp.arange(seq_len, dtype=jnp.int32)
    allowed = (row_ids[None, :] <= row_ids[:, None]) | (row_ids[None, :] < prefix_len)
    return jnp.where(allowed, scores, -1e30), grouped


def attend_forward(query, keys, values, prefix_len):
    scores, _ = masked_scores(query, keys, prefix_len)
    highest = jnp.max(scores, axis=-1, keepdims=True)
    shifted = jnp.exp(scores - highest)
    summed = jnp.sum(shifted, axis=-1, keepdims=True)
    weights = (shifted / summed).astype(bf16)
    output = jnp.einsum("hgqk,khd->qhgd", weights, values, preferred_element_type=f32)
    return output.reshape(query.shape[0], -1).astype(bf16), highest + jnp.log(summed)


def attend_backward(query, keys, values, grad_mixed, log_total, prefix_len):
    scores, grouped = masked_scores(query, keys, prefix_len)
    weights = jnp.exp(scores - log_total)
    seq_len, heads_kv, head_size = keys.shape
    grad_grouped = grad_mixed.reshape(seq_len, heads_kv, -1, head_size)
    grad_weights = jnp.einsum(
        "qhgd,khd->hgqk", grad_grouped, values, preferred_element_type=f32
    )
    grad_scores = (
        weights * (grad_weights - jnp.sum(weights * grad_weights, axis=-1, keepdims=True))
    ).astype(bf16)
    scaling = head_size ** (-0.5)
    grad_query = (
        jnp.einsum("hgqk,khd->qhgd", grad_scores, keys, preferred_element_type=f32) * scaling
    )
    grad_keys = (
        jnp.einsum("hgqk,qhgd->khd", grad_scores, grouped, preferred_element_type=f32) * scaling
    )
    grad_values = jnp.einsum(
        "hgqk,qhgd->khd", weights.astype(bf16), grad_grouped, preferred_element_type=f32
    )
    return grad_query.reshape(seq_len, -1, head_size), grad_keys, grad_values


def swap(values, axis, size, bit):
    return lax.ppermute(values, axis, [(m, m ^ bit) for m in range(size)])


def gather_line(block, axis, size):
    me = lax.axis_index(axis)
    up, down = [block], [block]
    for _ in range(1, size):
        up.append(lax.ppermute(up[-1], axis, [(m, m + 1) for m in range(size - 1)]))
        down.append(lax.ppermute(down[-1], axis, [(m + 1, m) for m in range(size - 1)]))
    return [block] + [jnp.where(me >= s, up[s], down[size - s]) for s in range(1, size)]


def tie(*values):
    return lax.optimization_barrier(values)


def by_rows(values):
    return with_layout_constraint(values, Layout(major_to_minor=(0, 1)))


def split(values):
    high = values.astype(bf16)
    return high, (values - high.astype(f32)).astype(bf16)


def put(result, piece, *starts):
    return lax.dynamic_update_slice(result, piece, starts)


def solution(mesh):
    n_dp, n_tensor = mesh.shape["dp"], mesh.shape["tensor"]
    inner = 4
    outer = n_dp // inner
    grid = Mesh(mesh.devices.reshape(inner, outer, n_tensor), ("i", "o", "t"))
    dp = ("i", "o")
    shared = ("i", "t")

    def to_owner_order(values):
        rows = values.shape[0]
        if outer == 1:
            return values
        split = jnp.swapaxes(values.reshape(rows, inner, outer, -1), 1, 2)
        if outer == 2:
            split = jnp.where(lax.axis_index("o") == 0, split, split[:, ::-1])
        return split.reshape(rows, -1)

    def from_owner_order(values):
        rows = values.shape[0]
        if outer == 1:
            return values
        split = values.reshape(rows, outer, inner, -1)
        if outer == 2:
            split = jnp.where(lax.axis_index("o") == 0, split, split[:, ::-1])
        return jnp.swapaxes(split, 1, 2).reshape(rows, -1)

    def pass_on(piece):
        if outer == 1:
            return piece[None]
        if outer == 2:
            return jnp.stack([piece, swap(piece, "o", 2, 1)])
        return lax.all_gather(piece, "o", axis=0)

    def sum_outer(parts):
        if outer == 1:
            return parts[0]
        if outer == 2:
            return (parts[0].astype(f32) + swap(parts[1], "o", 2, 1).astype(f32)).astype(bf16)
        return lax.psum_scatter(parts, "o", scatter_dimension=0, tiled=False)

    def share(block):
        rows, width = block.shape
        if n_tensor != 4:
            return lax.all_gather(block, shared, axis=0, tiled=True)
        me_i, me_t = lax.axis_index("i"), lax.axis_index("t")
        result = jnp.zeros((inner * n_tensor * rows, width), block.dtype)
        for shift, near in enumerate(gather_line(block, "i", inner)):
            pair = jnp.concatenate([near, swap(near, "t", n_tensor, 2)], axis=0)
            for bit, part in ((0, pair), (1, swap(pair, "t", n_tensor, 1))):
                place = (me_i - shift) % inner * n_tensor + (me_t ^ bit)
                result = put(result, part[:rows], place * rows, 0)
                result = put(result, part[rows:], (place ^ 2) * rows, 0)
        return result

    def sum_across(values):
        rows, width = values.shape[0] // (inner * n_tensor), values.shape[1]
        me_i, me_t = lax.axis_index("i"), lax.axis_index("t")
        blocks = values.reshape(inner, 2, 2, rows, width)
        result = []
        for shift in range(inner):
            block = lax.dynamic_index_in_dim(blocks, (me_i + shift) % inner, 0, keepdims=False)
            for axis, bit, own in ((1, 1, me_t % 2), (0, 2, me_t // 2)):
                keep = lax.dynamic_index_in_dim(block, own, axis, keepdims=False)
                send = lax.dynamic_index_in_dim(block, 1 - own, axis, keepdims=False)
                got = swap(send, "t", n_tensor, bit)
                block = (keep.astype(f32) + got.astype(f32)).astype(bf16)
            result.append(block)
        return result

    def sum_line(parts):
        total = parts[0].astype(f32)
        for shift in range(1, inner):
            pairs = [(m, (m + shift) % inner) for m in range(inner)]
            total = total + lax.ppermute(parts[shift], "i", pairs).astype(f32)
        return total

    def sum_tensor(values):
        if n_tensor != 4:
            return lax.psum(values, "t")
        for bit in (1, 2):
            values = values + swap(values, "t", n_tensor, bit)
        return values

    def on_device(
        tokens,
        cotangent,
        prefix,
        routes,
        norm1,
        w_query,
        w_key,
        w_value,
        w_out,
        norm2,
        w_router,
        w_gate,
        w_up,
        w_down,
    ):
        rows, width = tokens.shape
        group = routes.shape[0]
        n_experts, depth, hidden = w_gate.shape
        own_experts = n_experts // inner
        own_hidden = own_experts * hidden
        q_cols, k_cols = w_query.shape[1], w_key.shape[1]
        qkv_cols = q_cols + 2 * k_cols
        attn_cols = qkv_cols + q_cols
        side_cols = -(-(2 * n_experts + 2) // LANES) * LANES
        gate_cols = -(-2 * n_experts // LANES) * LANES
        me_i, me_t = lax.axis_index("i"), lax.axis_index("t")

        side = jnp.concatenate(
            [
                w_router,
                norm1[:, None],
                norm2[:, None],
                jnp.zeros((depth, side_cols - n_experts - 2), bf16),
            ],
            axis=1,
        )
        pack = jnp.concatenate([w_query, w_key, w_value, w_out.T, side], axis=1)
        tokens_all = lax.all_gather(tokens, "t", axis=0, tiled=True).astype(f32)
        packed = lax.all_gather(pack, dp, axis=0, tiled=True)

        def expert_piece(target):
            first = target * own_experts
            parts = [
                jnp.swapaxes(lax.dynamic_slice_in_dim(w, first, own_experts, 0), 0, 1)
                for w in (w_gate, w_up)
            ]
            down = lax.dynamic_slice_in_dim(w_down, first, own_experts, 0)
            parts.append(down.transpose(2, 0, 1))
            return jnp.concatenate([p.reshape(depth, own_hidden) for p in parts], axis=1)

        def to_owner(piece, shift):
            return lax.ppermute(piece, "i", [(m, (m + shift) % inner) for m in range(inner)])

        pieces = [expert_piece((me_i + shift) % inner) for shift in range(inner)]
        pieces[0], pieces[1], tokens_all = tie(pieces[0], pieces[1], tokens_all)
        owned = [pass_on(pieces[0])]
        near = to_owner(pieces[1], 1)
        pieces[2], pieces[3], owned[0], near, packed = tie(
            pieces[2], pieces[3], owned[0], near, packed
        )
        owned.append(pass_on(near))

        w_qkv = packed[:, :qkv_cols]
        w_out_t = packed[:, qkv_cols:attn_cols]
        router = packed[:, attn_cols : attn_cols + n_experts]
        gains = packed[:, attn_cols + n_experts : attn_cols + n_experts + 2].astype(f32).T
        gain_one, gain_two = gains[0], gains[1]

        normal_all = tokens_all * rms_scale(tokens_all)
        normed_one = (normal_all * gain_one).astype(bf16)
        cosine, sine = rotary_tables(group, HEAD_DIM // 2)
        qkv = jnp.dot(normed_one, w_qkv, preferred_element_type=f32)
        query = rotate(qkv[:, :q_cols].reshape(group, -1, HEAD_DIM), cosine, sine).astype(bf16)
        keys = rotate(
            qkv[:, q_cols : q_cols + k_cols].reshape(group, -1, HEAD_DIM), cosine, sine
        ).astype(bf16)
        values = qkv[:, q_cols + k_cols :].astype(bf16).reshape(group, -1, HEAD_DIM)
        attended, log_total = attend_forward(query, keys, values, prefix[0])
        near = to_owner(pieces[2], 2)
        pieces[3], attended = tie(pieces[3], attended)
        branch = lax.dot_general(
            attended, w_out_t, (((1,), (1,)), ((), ())), preferred_element_type=f32
        ).astype(bf16)
        tokens_f = tokens.astype(f32)
        branch = lax.psum_scatter(branch, "t", scatter_dimension=0, tiled=True)
        last = to_owner(pieces[3], 3)
        near, owned[1], branch = tie(near, owned[1], branch)
        owned += [pass_on(near), pass_on(last)]
        middle = tokens_f + branch.astype(f32)
        scale_two = rms_scale(middle)
        normed_two = (middle * scale_two * gain_two).astype(bf16)

        logits = jnp.dot(normed_two, router, preferred_element_type=f32)
        own_routes = lax.dynamic_slice_in_dim(routes, me_t * rows, rows, 0)
        expert_ids = jnp.arange(n_experts, dtype=jnp.int32)
        routed = jnp.any(own_routes[:, :, None] == expert_ids[None, None, :], axis=1)
        gates = jnp.where(routed, jax.nn.softmax(jnp.where(routed, logits, -1e30), axis=-1), 0.0)
        gates_high = gates.astype(bf16)
        gates_low = (gates - gates_high.astype(f32)).astype(bf16)
        shipped = jnp.concatenate(
            [
                to_owner_order(normed_two),
                gates_high,
                gates_low,
                jnp.zeros((rows, gate_cols - 2 * n_experts), bf16),
            ],
            axis=1,
        )
        shared_all = by_rows(lax.all_gather(by_rows(shipped), shared, axis=0, tiled=True))
        w_owned = jnp.zeros((outer, inner, depth, 3 * own_hidden), bf16)
        for shift in range(inner):
            w_owned = put(w_owned, owned[shift][:, None], 0, (me_i - shift) % inner, 0, 0)
        w_owned = w_owned.reshape(outer * inner * depth, 3 * own_hidden)
        cot_order, shared_all, w_owned = tie(by_rows(to_owner_order(cotangent)), shared_all, w_owned)
        w_gate_up, w_down_t = w_owned[:, : 2 * own_hidden], w_owned[:, 2 * own_hidden :]
        cot_all = by_rows(share(cot_order))
        count = shared_all.shape[0]
        normed_all = shared_all[:, :width]

        slot = jnp.arange(gate_cols, dtype=jnp.int32)[:, None]
        owner = me_i * own_experts + jnp.arange(own_hidden, dtype=jnp.int32)[None, :] // hidden
        spread = ((slot == owner) | (slot == owner + n_experts)).astype(bf16)
        gate_wide = jnp.dot(shared_all[:, width:], spread, preferred_element_type=f32)
        gate_up = jnp.dot(normed_all, w_gate_up, preferred_element_type=f32)
        gate_part, up_part = gate_up[:, :own_hidden], gate_up[:, own_hidden:]
        sigmoid_g = jax.nn.sigmoid(gate_part)
        silu_g = gate_part * sigmoid_g
        act = silu_g * up_part
        gated = (act * gate_wide).astype(bf16)
        expert_part = lax.dot_general(
            gated, w_down_t, (((1,), (1,)), ((), ())), preferred_element_type=f32
        ).astype(bf16)
        expert_part, cot_all = tie(by_rows(expert_part), cot_all)
        if n_tensor == 4:
            share_parts = sum_across(expert_part)
        else:
            share_parts = [lax.psum_scatter(expert_part, shared, scatter_dimension=0, tiled=True)]
        contract_rows = (((0,), (0,)), ((), ()))

        def to_sum(grad):
            by_owner = grad.reshape(outer, inner, depth, -1)
            return [
                sum_outer(
                    lax.dynamic_index_in_dim(by_owner, (me_i + shift) % inner, 1, keepdims=False)
                )
                for shift in range(inner)
            ]

        cot_part = jnp.dot(cot_all, w_down_t, preferred_element_type=f32)
        grad_act = cot_part * gate_wide
        grad_gate_up = jnp.concatenate(
            [
                (grad_act * up_part * sigmoid_g * (1.0 + gate_part * (1.0 - sigmoid_g))).astype(
                    bf16
                ),
                (grad_act * silu_g).astype(bf16),
            ],
            axis=1,
        )
        grad_gates = jnp.sum((act * cot_part).reshape(count, own_experts, hidden), axis=-1)
        gate_block = lax.dynamic_update_slice(
            jnp.zeros((count, side_cols), f32), grad_gates, (0, me_i * own_experts)
        )
        grad_normed_part = lax.dot_general(
            grad_gate_up, w_gate_up, (((1,), (1,)), ((), ())), preferred_element_type=f32
        )
        gates_back = lax.psum_scatter(
            gate_block.astype(bf16), shared, scatter_dimension=0, tiled=True
        )
        grad_normed_part, share_parts, gates_back = tie(
            by_rows(grad_normed_part.astype(bf16)), share_parts, gates_back
        )
        grad_back = lax.psum_scatter(grad_normed_part, shared, scatter_dimension=0, tiled=True)
        cot_rows, normed_rows, _ = tie(cot_all, normed_all, grad_normed_part)
        grad_w_down = lax.dot_general(
            cot_rows, gated, contract_rows, preferred_element_type=f32
        ).astype(bf16)
        grad_w_down, normed_rows = tie(grad_w_down, normed_rows)
        down_sums = to_sum(grad_w_down)
        grad_w_gate_up = lax.dot_general(
            normed_rows, grad_gate_up, contract_rows, preferred_element_type=f32
        ).astype(bf16)
        gate_up_sums = to_sum(grad_w_gate_up)
        sent_down = down_sums[:1] + [to_owner(down_sums[s], s) for s in range(1, inner)]
        sent_gate_up = gate_up_sums[:1] + [to_owner(gate_up_sums[s], s) for s in range(1, inner)]
        if n_tensor == 4:
            expert_share = sum_line(share_parts)
        else:
            expert_share = share_parts[0].astype(f32)
        sent_down, gate_up_sums, expert_share, grad_back = tie(
            sent_down, gate_up_sums, expert_share, grad_back
        )
        sent_gate_up[0] = gate_up_sums[0]
        mixed = (middle + from_owner_order(expert_share)).astype(bf16)

        grad_back = grad_back.astype(f32)
        grad_chosen = gates_back[:, :n_experts].astype(f32)
        grad_logits = gates * (
            grad_chosen - jnp.sum(gates * grad_chosen, axis=-1, keepdims=True)
        )
        grad_normed_two = from_owner_order(grad_back) + jnp.dot(
            grad_logits, router.astype(f32).T, precision=HIGHEST
        )
        grad_middle_part, normal_two = norm_backward(
            middle, scale_two, gain_two, grad_normed_two
        )
        grad_middle = cotangent.astype(f32) + grad_middle_part
        grad_gain_two = jnp.sum(grad_normed_two * normal_two, axis=0)
        grad_router_part = lax.dot_general(
            normed_two.astype(f32), grad_logits, contract_rows, precision=HIGHEST
        )
        grad_branch = lax.all_gather(grad_middle.astype(bf16), "t", axis=0, tiled=True)
        grad_out_part = lax.dot_general(
            grad_branch, attended, contract_rows, preferred_element_type=f32
        ).astype(bf16)
        grad_out_part, sent_gate_up[1], grad_branch = tie(
            jnp.concatenate(
                [
                    grad_out_part,
                    *split(jnp.concatenate([grad_router_part, grad_gain_two[:, None]], axis=1)),
                    jnp.zeros((width, side_cols - 2 * n_experts - 2), bf16),
                ],
                axis=1,
            ),
            sent_gate_up[1],
            grad_branch,
        )
        shard_out = lax.psum_scatter(grad_out_part, dp, scatter_dimension=0, tiled=True)
        grad_attended = jnp.dot(
            grad_branch, w_out_t, preferred_element_type=f32
        ).astype(bf16)
        grad_query, grad_keys, grad_values = attend_backward(
            query, keys, values, grad_attended, log_total, prefix[0]
        )
        grad_qkv = jnp.concatenate(
            [
                rotate(grad_query, cosine, -sine).astype(bf16).reshape(group, -1),
                rotate(grad_keys, cosine, -sine).astype(bf16).reshape(group, -1),
                grad_values.astype(bf16).reshape(group, -1),
            ],
            axis=1,
        )
        grad_normed_one = lax.dot_general(
            grad_qkv, w_qkv, (((1,), (1,)), ((), ())), preferred_element_type=f32
        )
        grad_gain_one = jnp.sum(grad_normed_one * normal_all, axis=0)
        own_grad_one = lax.psum_scatter(
            grad_normed_one.astype(bf16), "t", scatter_dimension=0, tiled=True
        ).astype(f32)
        grad_input_part, _ = norm_backward(tokens_f, rms_scale(tokens_f), gain_one, own_grad_one)
        grad_tokens = grad_middle + grad_input_part

        grad_attn = jnp.concatenate(
            [
                lax.dot_general(
                    normed_one, grad_qkv, contract_rows, preferred_element_type=f32
                ).astype(bf16),
                *split(grad_gain_one[:, None]),
                jnp.zeros((width, LANES - 2), bf16),
            ],
            axis=1,
        )
        grad_attn, own_grad_one, shard_out, sent_gate_up[2] = tie(
            grad_attn, own_grad_one, shard_out, sent_gate_up[2]
        )
        shard_attn = lax.psum_scatter(grad_attn, dp, scatter_dimension=0, tiled=True).astype(f32)
        gain_sum = sum_tensor(shard_attn[:, qkv_cols] + shard_attn[:, qkv_cols + 1])
        shard_out = shard_out.astype(f32)
        side_sum = shard_out[:, q_cols : q_cols + 2 * (n_experts + 1)].reshape(depth, 2, -1)
        side_sum = sum_tensor(jnp.sum(side_sum, axis=1))

        grad_gate = jnp.zeros((n_experts, depth, hidden), f32)
        grad_up, grad_down = grad_gate, jnp.zeros((n_experts, hidden, depth), f32)
        for shift in range(inner):
            start = (me_i - shift) % inner * own_experts
            part = sent_down[shift]
            part = part.reshape(depth, own_experts, hidden).transpose(1, 2, 0)
            grad_down = put(grad_down, part.astype(f32), start, 0, 0)
            part = sent_gate_up[shift]
            part = part.reshape(depth, 2, own_experts, hidden).transpose(1, 2, 0, 3).astype(f32)
            grad_gate = put(grad_gate, part[0], start, 0, 0)
            grad_up = put(grad_up, part[1], start, 0, 0)
        return (
            mixed,
            grad_tokens,
            gain_sum,
            shard_attn[:, :q_cols],
            shard_attn[:, q_cols : q_cols + k_cols],
            shard_attn[:, q_cols + k_cols : qkv_cols],
            shard_out[:, :q_cols].T,
            side_sum[:, n_experts],
            side_sum[:, :n_experts],
            grad_gate,
            grad_up,
            grad_down,
        )

    in_specs = (
        P(("i", "o", "t"), None),
        P(("i", "o", "t"), None),
        P(dp),
        P(dp, None),
        P(dp),
        P(dp, "t"),
        P(dp, "t"),
        P(dp, "t"),
        P("t", dp),
        P(dp),
        P(dp, None),
        P(None, dp, "t"),
        P(None, dp, "t"),
        P(None, "t", dp),
    )
    out_specs = (
        P(("i", "o", "t"), None),
        P(("i", "o", "t"), None),
        P(dp),
        P(dp, "t"),
        P(dp, "t"),
        P(dp, "t"),
        P("t", dp),
        P(dp),
        P(dp, None),
        P(None, dp, "t"),
        P(None, dp, "t"),
        P(None, "t", dp),
    )
    return jax.shard_map(
        on_device, mesh=grid, in_specs=in_specs, out_specs=out_specs, check_vma=False
    )
```

```python
import jax
import jax.numpy as jnp
from jax import lax
from jax.experimental.layout import Layout, with_layout_constraint
from jax.sharding import Mesh, PartitionSpec as P

HEAD_DIM = 64
EPSILON = 1e-05
LANES = 128
HIGHEST = lax.Precision.HIGHEST
f32 = jnp.float32
bf16 = jnp.bfloat16


def rms_scale(values):
    return lax.rsqrt(jnp.mean(values * values, axis=-1, keepdims=True) + EPSILON)


def norm_backward(values, scale, gain, grad_normed):
    normal_x = values * scale
    grad_hat = grad_normed * gain
    grad_values = scale * (
        grad_hat - normal_x * jnp.mean(grad_hat * normal_x, axis=-1, keepdims=True)
    )
    return grad_values, normal_x


def rotary_tables(row_count, half):
    position = jnp.arange(row_count, dtype=jnp.int32).astype(f32)
    inverse = jnp.power(10000.0, -jnp.arange(half, dtype=jnp.int32).astype(f32) / half)
    angle = position[:, None] * inverse[None, :]
    return jnp.cos(angle)[:, None, :], jnp.sin(angle)[:, None, :]


def rotate(tensor, cosine, sine):
    half = tensor.shape[-1] // 2
    first = tensor[..., :half]
    second = tensor[..., half:]
    return jnp.concatenate(
        [first * cosine - second * sine, second * cosine + first * sine], axis=-1
    )


def tie(*values):
    return lax.optimization_barrier(values)


def masked_scores(query, keys, prefix_len):
    seq_len, heads_kv, head_size = keys.shape
    grouped = query.reshape(seq_len, heads_kv, -1, head_size)
    scores = jnp.einsum(
        "qhgd,khd->hgqk", grouped, keys, preferred_element_type=f32
    ) * head_size ** (-0.5)
    row_ids = jnp.arange(seq_len, dtype=jnp.int32)
    allowed = (row_ids[None, :] <= row_ids[:, None]) | (row_ids[None, :] < prefix_len)
    return jnp.where(allowed, scores, -1e30), grouped


def attend_forward(query, keys, values, prefix_len):
    scores, _ = masked_scores(query, keys, prefix_len)
    highest = jnp.max(scores, axis=-1, keepdims=True)
    shifted = jnp.exp(scores - highest)
    summed = jnp.sum(shifted, axis=-1, keepdims=True)
    weights = (shifted / summed).astype(bf16)
    output = jnp.einsum("hgqk,khd->qhgd", weights, values, preferred_element_type=f32)
    return output.reshape(query.shape[0], -1).astype(bf16), highest + jnp.log(summed)


def attend_backward(query, keys, values, grad_mixed, log_total, prefix_len, hold):
    scores, grouped = masked_scores(query, keys, prefix_len)
    weights = jnp.exp(scores - log_total)
    seq_len, heads_kv, head_size = keys.shape
    grad_grouped = grad_mixed.reshape(seq_len, heads_kv, -1, head_size)
    grad_weights = jnp.einsum(
        "qhgd,khd->hgqk", grad_grouped, values, preferred_element_type=f32
    )
    grad_scores = (
        weights * (grad_weights - jnp.sum(weights * grad_weights, axis=-1, keepdims=True))
    ).astype(bf16)
    grad_scores, hold = tie(grad_scores, hold)
    scaling = head_size ** (-0.5)
    grad_query = (
        jnp.einsum("hgqk,khd->qhgd", grad_scores, keys, preferred_element_type=f32) * scaling
    )
    grad_keys = (
        jnp.einsum("hgqk,qhgd->khd", grad_scores, grouped, preferred_element_type=f32) * scaling
    )
    grad_values = jnp.einsum(
        "hgqk,qhgd->khd", weights.astype(bf16), grad_grouped, preferred_element_type=f32
    )
    return grad_query.reshape(seq_len, -1, head_size), grad_keys, grad_values, hold


def swap(values, axis, size, bit):
    return lax.ppermute(values, axis, [(m, m ^ bit) for m in range(size)])


def by_rows(values):
    return with_layout_constraint(values, Layout(major_to_minor=(0, 1)))


def split(values):
    high = values.astype(bf16)
    return high, (values - high.astype(f32)).astype(bf16)


def put(result, piece, *starts):
    return lax.dynamic_update_slice(result, piece, starts)


def solution(mesh):
    n_dp, n_tensor = mesh.shape["dp"], mesh.shape["tensor"]
    inner = 4
    outer = n_dp // inner
    grid = Mesh(mesh.devices.reshape(inner, outer, n_tensor), ("i", "o", "t"))
    dp = ("i", "o")
    shared = ("i", "t")

    def to_owner_order(values):
        rows = values.shape[0]
        if outer == 1:
            return values
        split = jnp.swapaxes(values.reshape(rows, inner, outer, -1), 1, 2)
        if outer == 2:
            split = jnp.where(lax.axis_index("o") == 0, split, split[:, ::-1])
        return split.reshape(rows, -1)

    def from_owner_order(values):
        rows = values.shape[0]
        if outer == 1:
            return values
        split = values.reshape(rows, outer, inner, -1)
        if outer == 2:
            split = jnp.where(lax.axis_index("o") == 0, split, split[:, ::-1])
        return jnp.swapaxes(split, 1, 2).reshape(rows, -1)

    def pass_on(pair):
        if outer == 2:
            return tuple(jnp.stack([piece, swap(piece, "o", 2, 1)]) for piece in pair)
        return tuple(lax.all_gather(piece, "o", axis=0) for piece in pair)

    def sum_outer(parts):
        if outer == 1:
            return parts[0]
        if outer == 2:
            return (parts[0].astype(f32) + swap(parts[1], "o", 2, 1).astype(f32)).astype(bf16)
        return lax.psum_scatter(parts, "o", scatter_dimension=0, tiled=False)

    def gather_t(block):
        if n_tensor != 4:
            return lax.all_gather(block, "t", axis=0, tiled=True)
        rows, width = block.shape
        me_t = lax.axis_index("t")
        result = jnp.zeros((n_tensor * rows, width), block.dtype)
        pair = jnp.concatenate([block, swap(block, "t", n_tensor, 2)], axis=0)
        for bit, part in ((0, pair), (1, swap(pair, "t", n_tensor, 1))):
            result = put(result, part[:rows], (me_t ^ bit) * rows, 0)
            result = put(result, part[rows:], (me_t ^ bit ^ 2) * rows, 0)
        return result

    def scatter_t(values):
        if n_tensor != 4:
            return lax.psum_scatter(values, "t", scatter_dimension=0, tiled=True).astype(f32)
        me_t = lax.axis_index("t")
        block = values.reshape(2, 2, -1, values.shape[1])
        for axis, bit, own in ((1, 1, me_t % 2), (0, 2, me_t // 2)):
            keep = lax.dynamic_index_in_dim(block, own, axis, keepdims=False)
            send = lax.dynamic_index_in_dim(block, 1 - own, axis, keepdims=False)
            block = keep.astype(f32) + swap(send.astype(bf16), "t", n_tensor, bit).astype(f32)
        return block

    def sum_tensor(values):
        if n_tensor != 4:
            return lax.psum(values, "t")
        for bit in (1, 2):
            values = values + swap(values, "t", n_tensor, bit)
        return values

    def on_device(
        tokens,
        cotangent,
        prefix,
        routes,
        norm1,
        w_query,
        w_key,
        w_value,
        w_out,
        norm2,
        w_router,
        w_gate,
        w_up,
        w_down,
    ):
        rows, width = tokens.shape
        group = routes.shape[0]
        n_experts, depth, hidden = w_gate.shape
        own_experts = n_experts // inner
        own_hidden = own_experts * hidden
        q_cols, k_cols = w_query.shape[1], w_key.shape[1]
        qkv_cols = q_cols + 2 * k_cols
        attn_cols = qkv_cols + q_cols
        side_cols = -(-(2 * n_experts + 2) // LANES) * LANES
        gate_cols = -(-2 * n_experts // LANES) * LANES
        me_i, me_t = lax.axis_index("i"), lax.axis_index("t")

        side = jnp.concatenate(
            [
                w_router,
                norm1[:, None],
                norm2[:, None],
                jnp.zeros((depth, side_cols - n_experts - 2), bf16),
            ],
            axis=1,
        )
        pack = jnp.concatenate([w_query, w_key, w_value, w_out.T, side], axis=1)
        tokens_all = lax.all_gather(tokens, "t", axis=0, tiled=True).astype(f32)
        packed = lax.all_gather(pack, dp, axis=0, tiled=True)

        def expert_piece(target):
            first = target * own_experts
            gate, up = (
                jnp.swapaxes(lax.dynamic_slice_in_dim(w, first, own_experts, 0), 0, 1)
                for w in (w_gate, w_up)
            )
            down = lax.dynamic_slice_in_dim(w_down, first, own_experts, 0).transpose(2, 0, 1)
            gate_up = jnp.concatenate(
                [gate.reshape(depth, own_hidden), up.reshape(depth, own_hidden)], axis=1
            )
            return gate_up, down.reshape(depth, own_hidden)

        def to_owner(piece, shift):
            pairs = [(m, (m + shift) % inner) for m in range(inner)]
            return jax.tree.map(lambda part: lax.ppermute(part, "i", pairs), piece)

        pieces = [expert_piece((me_i + shift) % inner) for shift in range(inner)]
        far_gate_up, far_down = to_owner(pieces[2], 2)
        far_down, tokens_all = tie(far_down, tokens_all)
        pieces[0], pieces[1], pieces[3], far_gate_up, packed = tie(
            pieces[0], pieces[1], pieces[3], far_gate_up, packed
        )
        near = to_owner(pieces[1], 1)
        owned = [pass_on(pieces[0])]

        w_qkv = packed[:, :qkv_cols]
        w_out_t = packed[:, qkv_cols:attn_cols]
        router = packed[:, attn_cols : attn_cols + n_experts]
        gains = packed[:, attn_cols + n_experts : attn_cols + n_experts + 2].astype(f32).T
        gain_one, gain_two = gains[0], gains[1]

        normal_all = tokens_all * rms_scale(tokens_all)
        normed_one = (normal_all * gain_one).astype(bf16)
        cosine, sine = rotary_tables(group, HEAD_DIM // 2)
        qkv = jnp.dot(normed_one, w_qkv, preferred_element_type=f32)
        query = rotate(qkv[:, :q_cols].reshape(group, -1, HEAD_DIM), cosine, sine).astype(bf16)
        keys = rotate(
            qkv[:, q_cols : q_cols + k_cols].reshape(group, -1, HEAD_DIM), cosine, sine
        ).astype(bf16)
        values = qkv[:, q_cols + k_cols :].astype(bf16).reshape(group, -1, HEAD_DIM)
        attended, log_total = attend_forward(query, keys, values, prefix[0])
        pieces[3], near, owned[0], attended = tie(pieces[3], near, owned[0], attended)
        last = to_owner(pieces[3], 3)
        branch = lax.dot_general(
            attended, w_out_t, (((1,), (1,)), ((), ())), preferred_element_type=f32
        ).astype(bf16)
        tokens_f = tokens.astype(f32)
        branch = lax.psum_scatter(branch, "t", scatter_dimension=0, tiled=True)
        far_gate_up, near, last, branch = tie(far_gate_up, near, last, branch)
        owned += [pass_on(near), pass_on((far_gate_up, far_down)), pass_on(last)]
        middle = tokens_f + branch.astype(f32)
        scale_two = rms_scale(middle)
        normed_two = (middle * scale_two * gain_two).astype(bf16)

        logits = jnp.dot(normed_two, router, preferred_element_type=f32)
        own_routes = lax.dynamic_slice_in_dim(routes, me_t * rows, rows, 0)
        expert_ids = jnp.arange(n_experts, dtype=jnp.int32)
        routed = jnp.any(own_routes[:, :, None] == expert_ids[None, None, :], axis=1)
        gates = jnp.where(routed, jax.nn.softmax(jnp.where(routed, logits, -1e30), axis=-1), 0.0)
        gates_high = gates.astype(bf16)
        gates_low = (gates - gates_high.astype(f32)).astype(bf16)
        shipped = jnp.concatenate(
            [
                to_owner_order(normed_two),
                gates_high,
                gates_low,
                jnp.zeros((rows, gate_cols - 2 * n_experts), bf16),
            ],
            axis=1,
        )
        shared_all = by_rows(lax.all_gather(by_rows(shipped), shared, axis=0, tiled=True))
        w_gate_up = jnp.zeros((outer, inner, depth, 2 * own_hidden), bf16)
        w_down_t = jnp.zeros((outer, inner, depth, own_hidden), bf16)
        for shift in range(inner):
            source = (me_i - shift) % inner
            w_gate_up = put(w_gate_up, owned[shift][0][:, None], 0, source, 0, 0)
            w_down_t = put(w_down_t, owned[shift][1][:, None], 0, source, 0, 0)
        cot_order, shared_all, w_gate_up, w_down_t = tie(
            by_rows(to_owner_order(cotangent)),
            shared_all,
            w_gate_up.reshape(outer * inner * depth, 2 * own_hidden),
            w_down_t.reshape(outer * inner * depth, own_hidden),
        )
        cot_all = by_rows(lax.all_gather(cot_order, shared, axis=0, tiled=True))
        count = shared_all.shape[0]
        normed_all = shared_all[:, :width]

        slot = jnp.arange(gate_cols, dtype=jnp.int32)[:, None]
        owner = me_i * own_experts + jnp.arange(own_hidden, dtype=jnp.int32)[None, :] // hidden
        spread = ((slot == owner) | (slot == owner + n_experts)).astype(bf16)
        gate_wide = jnp.dot(shared_all[:, width:], spread, preferred_element_type=f32)
        gate_up = jnp.dot(normed_all, w_gate_up, preferred_element_type=f32)
        gate_part, up_part = gate_up[:, :own_hidden], gate_up[:, own_hidden:]
        sigmoid_g = jax.nn.sigmoid(gate_part)
        silu_g = gate_part * sigmoid_g
        act = silu_g * up_part
        gated = (act * gate_wide).astype(bf16)
        expert_part = lax.dot_general(
            gated, w_down_t, (((1,), (1,)), ((), ())), preferred_element_type=f32
        ).astype(bf16)
        expert_part, cot_all = tie(by_rows(expert_part), cot_all)
        expert_share = lax.psum_scatter(expert_part, shared, scatter_dimension=0, tiled=True)
        contract_rows = (((0,), (0,)), ((), ()))
        grad_w_down = lax.dot_general(
            cot_all, gated, contract_rows, preferred_element_type=f32
        ).astype(bf16)
        grad_w_down, cot_all = tie(grad_w_down, cot_all)

        def to_sum(grad):
            by_owner = grad.reshape(outer, inner, depth, -1)
            return [
                sum_outer(
                    lax.dynamic_index_in_dim(by_owner, (me_i + shift) % inner, 1, keepdims=False)
                )
                for shift in range(inner)
            ]

        down_sums = to_sum(grad_w_down)
        cot_part = jnp.dot(cot_all, w_down_t, preferred_element_type=f32)
        grad_act = cot_part * gate_wide
        grad_gate_up = jnp.concatenate(
            [
                (grad_act * up_part * sigmoid_g * (1.0 + gate_part * (1.0 - sigmoid_g))).astype(
                    bf16
                ),
                (grad_act * silu_g).astype(bf16),
            ],
            axis=1,
        )
        grad_gates = jnp.sum((act * cot_part).reshape(count, own_experts, hidden), axis=-1)
        gate_block = lax.dynamic_update_slice(
            jnp.zeros((count, side_cols), f32), grad_gates, (0, me_i * own_experts)
        )
        grad_normed_part = lax.dot_general(
            grad_gate_up, w_gate_up, (((1,), (1,)), ((), ())), preferred_element_type=f32
        )
        grad_shipped = jnp.concatenate([grad_normed_part, gate_block], axis=1).astype(bf16)
        grad_shipped, down_sums, expert_share = tie(by_rows(grad_shipped), down_sums, expert_share)
        grad_back = lax.psum_scatter(grad_shipped, shared, scatter_dimension=0, tiled=True)
        normed_rows, _ = tie(normed_all, grad_shipped)
        grad_w_gate_up = lax.dot_general(
            normed_rows, grad_gate_up, contract_rows, preferred_element_type=f32
        ).astype(bf16)
        gate_up_sums = to_sum(grad_w_gate_up)
        gate_up_sums, down_sums, grad_back = tie(gate_up_sums, down_sums, grad_back)
        sent_down = down_sums[:1] + [to_owner(down_sums[s], s) for s in range(1, inner)]
        sent_gate_up = gate_up_sums[:1] + [to_owner(gate_up_sums[s], s) for s in range(1, inner)]
        mixed = (middle + from_owner_order(expert_share).astype(f32)).astype(bf16)

        grad_back = grad_back.astype(f32)
        grad_chosen = grad_back[:, width : width + n_experts]
        grad_logits = gates * (
            grad_chosen - jnp.sum(gates * grad_chosen, axis=-1, keepdims=True)
        )
        grad_normed_two = from_owner_order(grad_back[:, :width]) + jnp.dot(
            grad_logits, router.astype(f32).T, precision=HIGHEST
        )
        grad_middle_part, normal_two = norm_backward(
            middle, scale_two, gain_two, grad_normed_two
        )
        grad_middle = cotangent.astype(f32) + grad_middle_part
        grad_gain_two = jnp.sum(grad_normed_two * normal_two, axis=0)
        grad_router_part = lax.dot_general(
            normed_two.astype(f32), grad_logits, contract_rows, precision=HIGHEST
        )
        grad_branch = gather_t(grad_middle.astype(bf16))
        grad_out_part = lax.dot_general(
            grad_branch, attended, contract_rows, preferred_element_type=f32
        ).astype(bf16)
        grad_out_part, sent_down[2], grad_branch = tie(
            jnp.concatenate(
                [
                    grad_out_part,
                    *split(jnp.concatenate([grad_router_part, grad_gain_two[:, None]], axis=1)),
                    jnp.zeros((width, side_cols - 2 * n_experts - 2), bf16),
                ],
                axis=1,
            ),
            sent_down[2],
            grad_branch,
        )
        shard_out = lax.psum_scatter(grad_out_part, dp, scatter_dimension=0, tiled=True)
        grad_attended = jnp.dot(
            grad_branch, w_out_t, preferred_element_type=f32
        ).astype(bf16)
        grad_query, grad_keys, grad_values, (sent_down[1], sent_down[3]) = attend_backward(
            query,
            keys,
            values,
            grad_attended,
            log_total,
            prefix[0],
            (sent_down[1], sent_down[3]),
        )
        grad_query, grad_keys, grad_values, shard_out, sent_gate_up[2] = tie(
            grad_query, grad_keys, grad_values, shard_out, sent_gate_up[2]
        )
        grad_qkv = jnp.concatenate(
            [
                rotate(grad_query, cosine, -sine).astype(bf16).reshape(group, -1),
                rotate(grad_keys, cosine, -sine).astype(bf16).reshape(group, -1),
                grad_values.astype(bf16).reshape(group, -1),
            ],
            axis=1,
        )
        grad_normed_one = lax.dot_general(
            grad_qkv, w_qkv, (((1,), (1,)), ((), ())), preferred_element_type=f32
        )
        grad_gain_one = jnp.sum(grad_normed_one * normal_all, axis=0)
        own_grad_one = scatter_t(grad_normed_one.astype(bf16))
        grad_input_part, _ = norm_backward(tokens_f, rms_scale(tokens_f), gain_one, own_grad_one)
        grad_tokens = grad_middle + grad_input_part

        grad_attn = jnp.concatenate(
            [
                lax.dot_general(
                    normed_one, grad_qkv, contract_rows, preferred_element_type=f32
                ).astype(bf16),
                *split(grad_gain_one[:, None]),
                jnp.zeros((width, LANES - 2), bf16),
            ],
            axis=1,
        )
        shard_attn = lax.psum_scatter(grad_attn, dp, scatter_dimension=0, tiled=True).astype(f32)
        gain_sum = sum_tensor(shard_attn[:, qkv_cols] + shard_attn[:, qkv_cols + 1])
        shard_out = shard_out.astype(f32)
        side_sum = shard_out[:, q_cols : q_cols + 2 * (n_experts + 1)].reshape(depth, 2, -1)
        side_sum = sum_tensor(jnp.sum(side_sum, axis=1))

        grad_gate = jnp.zeros((n_experts, depth, hidden), f32)
        grad_up, grad_down = grad_gate, jnp.zeros((n_experts, hidden, depth), f32)
        for shift in range(inner):
            start = (me_i - shift) % inner * own_experts
            part = sent_down[shift]
            part = part.reshape(depth, own_experts, hidden).transpose(1, 2, 0)
            grad_down = put(grad_down, part.astype(f32), start, 0, 0)
            part = sent_gate_up[shift]
            part = part.reshape(depth, 2, own_experts, hidden).transpose(1, 2, 0, 3).astype(f32)
            grad_gate = put(grad_gate, part[0], start, 0, 0)
            grad_up = put(grad_up, part[1], start, 0, 0)
        return (
            mixed,
            grad_tokens,
            gain_sum,
            shard_attn[:, :q_cols],
            shard_attn[:, q_cols : q_cols + k_cols],
            shard_attn[:, q_cols + k_cols : qkv_cols],
            shard_out[:, :q_cols].T,
            side_sum[:, n_experts],
            side_sum[:, :n_experts],
            grad_gate,
            grad_up,
            grad_down,
        )

    in_specs = (
        P(("i", "o", "t"), None),
        P(("i", "o", "t"), None),
        P(dp),
        P(dp, None),
        P(dp),
        P(dp, "t"),
        P(dp, "t"),
        P(dp, "t"),
        P("t", dp),
        P(dp),
        P(dp, None),
        P(None, dp, "t"),
        P(None, dp, "t"),
        P(None, "t", dp),
    )
    out_specs = (
        P(("i", "o", "t"), None),
        P(("i", "o", "t"), None),
        P(dp),
        P(dp, "t"),
        P(dp, "t"),
        P(dp, "t"),
        P("t", dp),
        P(dp),
        P(dp, None),
        P(None, dp, "t"),
        P(None, dp, "t"),
        P(None, "t", dp),
    )
    return jax.shard_map(
        on_device, mesh=grid, in_specs=in_specs, out_specs=out_specs, check_vma=False
    )
```

```python
import jax
import jax.numpy as jnp
from jax import lax
from jax.experimental.layout import Layout, with_layout_constraint
from jax.sharding import Mesh, PartitionSpec as P

HEAD_DIM = 64
EPSILON = 1e-05
LANES = 128
HIGHEST = lax.Precision.HIGHEST
f32 = jnp.float32
bf16 = jnp.bfloat16


def rms_scale(values):
    return lax.rsqrt(jnp.mean(values * values, axis=-1, keepdims=True) + EPSILON)


def norm_backward(values, scale, gain, grad_normed):
    normal_x = values * scale
    grad_hat = grad_normed * gain
    grad_values = scale * (
        grad_hat - normal_x * jnp.mean(grad_hat * normal_x, axis=-1, keepdims=True)
    )
    return grad_values, normal_x


def rotary_tables(row_count, half):
    position = jnp.arange(row_count, dtype=jnp.int32).astype(f32)
    inverse = jnp.power(10000.0, -jnp.arange(half, dtype=jnp.int32).astype(f32) / half)
    angle = position[:, None] * inverse[None, :]
    return jnp.cos(angle)[:, None, :], jnp.sin(angle)[:, None, :]


def rotate(tensor, cosine, sine):
    half = tensor.shape[-1] // 2
    first = tensor[..., :half]
    second = tensor[..., half:]
    return jnp.concatenate(
        [first * cosine - second * sine, second * cosine + first * sine], axis=-1
    )


def tie(*values):
    return lax.optimization_barrier(values)


def masked_scores(query, keys, prefix_len):
    seq_len, heads_kv, head_size = keys.shape
    grouped = query.reshape(seq_len, heads_kv, -1, head_size)
    scores = jnp.einsum(
        "qhgd,khd->hgqk", grouped, keys, preferred_element_type=f32
    ) * head_size ** (-0.5)
    row_ids = jnp.arange(seq_len, dtype=jnp.int32)
    allowed = (row_ids[None, :] <= row_ids[:, None]) | (row_ids[None, :] < prefix_len)
    return jnp.where(allowed, scores, -1e30), grouped


def attend_forward(query, keys, values, prefix_len):
    scores, _ = masked_scores(query, keys, prefix_len)
    highest = jnp.max(scores, axis=-1, keepdims=True)
    shifted = jnp.exp(scores - highest)
    summed = jnp.sum(shifted, axis=-1, keepdims=True)
    weights = (shifted / summed).astype(bf16)
    output = jnp.einsum("hgqk,khd->qhgd", weights, values, preferred_element_type=f32)
    return output.reshape(query.shape[0], -1).astype(bf16), highest + jnp.log(summed)


def attend_backward(query, keys, values, grad_mixed, log_total, prefix_len, hold):
    scores, grouped = masked_scores(query, keys, prefix_len)
    weights = jnp.exp(scores - log_total)
    seq_len, heads_kv, head_size = keys.shape
    grad_grouped = grad_mixed.reshape(seq_len, heads_kv, -1, head_size)
    grad_weights = jnp.einsum(
        "qhgd,khd->hgqk", grad_grouped, values, preferred_element_type=f32
    )
    grad_scores = (
        weights * (grad_weights - jnp.sum(weights * grad_weights, axis=-1, keepdims=True))
    ).astype(bf16)
    grad_scores, hold = tie(grad_scores, hold)
    scaling = head_size ** (-0.5)
    grad_query = (
        jnp.einsum("hgqk,khd->qhgd", grad_scores, keys, preferred_element_type=f32) * scaling
    )
    grad_keys = (
        jnp.einsum("hgqk,qhgd->khd", grad_scores, grouped, preferred_element_type=f32) * scaling
    )
    grad_values = jnp.einsum(
        "hgqk,qhgd->khd", weights.astype(bf16), grad_grouped, preferred_element_type=f32
    )
    return grad_query.reshape(seq_len, -1, head_size), grad_keys, grad_values, hold


def swap(values, axis, size, bit):
    return lax.ppermute(values, axis, [(m, m ^ bit) for m in range(size)])


def by_rows(values):
    return with_layout_constraint(values, Layout(major_to_minor=(0, 1)))


def split(values):
    high = values.astype(bf16)
    return high, (values - high.astype(f32)).astype(bf16)


def put(result, piece, *starts):
    return lax.dynamic_update_slice(result, piece, starts)


def solution(mesh):
    n_dp, n_tensor = mesh.shape["dp"], mesh.shape["tensor"]
    inner = 4
    outer = n_dp // inner
    grid = Mesh(mesh.devices.reshape(inner, outer, n_tensor), ("i", "o", "t"))
    dp = ("i", "o")
    shared = ("i", "t")

    def to_owner_order(values):
        rows = values.shape[0]
        if outer == 1:
            return values
        split = jnp.swapaxes(values.reshape(rows, inner, outer, -1), 1, 2)
        if outer == 2:
            split = jnp.where(lax.axis_index("o") == 0, split, split[:, ::-1])
        return split.reshape(rows, -1)

    def from_owner_order(values):
        rows = values.shape[0]
        if outer == 1:
            return values
        split = values.reshape(rows, outer, inner, -1)
        if outer == 2:
            split = jnp.where(lax.axis_index("o") == 0, split, split[:, ::-1])
        return jnp.swapaxes(split, 1, 2).reshape(rows, -1)

    def pass_on(pair):
        if outer == 2:
            return tuple(jnp.stack([piece, swap(piece, "o", 2, 1)]) for piece in pair)
        return tuple(lax.all_gather(piece, "o", axis=0) for piece in pair)

    def sum_outer(parts):
        if outer == 1:
            return parts[0]
        if outer == 2:
            return (parts[0].astype(f32) + swap(parts[1], "o", 2, 1).astype(f32)).astype(bf16)
        return lax.psum_scatter(parts, "o", scatter_dimension=0, tiled=False)

    def gather_t(block):
        if n_tensor != 4:
            return lax.all_gather(block, "t", axis=0, tiled=True)
        rows, width = block.shape
        me_t = lax.axis_index("t")
        result = jnp.zeros((n_tensor * rows, width), block.dtype)
        pair = jnp.concatenate([block, swap(block, "t", n_tensor, 2)], axis=0)
        for bit, part in ((0, pair), (1, swap(pair, "t", n_tensor, 1))):
            result = put(result, part[:rows], (me_t ^ bit) * rows, 0)
            result = put(result, part[rows:], (me_t ^ bit ^ 2) * rows, 0)
        return result

    def scatter_t(values):
        if n_tensor != 4:
            return lax.psum_scatter(values, "t", scatter_dimension=0, tiled=True).astype(f32)
        me_t = lax.axis_index("t")
        block = values.reshape(2, 2, -1, values.shape[1])
        for axis, bit, own in ((1, 1, me_t % 2), (0, 2, me_t // 2)):
            keep = lax.dynamic_index_in_dim(block, own, axis, keepdims=False)
            send = lax.dynamic_index_in_dim(block, 1 - own, axis, keepdims=False)
            block = keep.astype(f32) + swap(send.astype(bf16), "t", n_tensor, bit).astype(f32)
        return block

    def sum_tensor(values):
        me_t = lax.axis_index("t")
        slots = put(jnp.zeros((n_tensor, *values.shape), f32), values[None], me_t, 0, 0)
        for shift in range(1, n_tensor):
            got = lax.ppermute(values, "t", [(m, (m + shift) % n_tensor) for m in range(n_tensor)])
            slots = put(slots, got[None], (me_t - shift) % n_tensor, 0, 0)
        return jnp.sum(slots, axis=0)

    def on_device(
        tokens,
        cotangent,
        prefix,
        routes,
        norm1,
        w_query,
        w_key,
        w_value,
        w_out,
        norm2,
        w_router,
        w_gate,
        w_up,
        w_down,
    ):
        rows, width = tokens.shape
        group = routes.shape[0]
        n_experts, depth, hidden = w_gate.shape
        own_experts = n_experts // inner
        own_hidden = own_experts * hidden
        q_cols, k_cols = w_query.shape[1], w_key.shape[1]
        qkv_cols = q_cols + 2 * k_cols
        attn_cols = qkv_cols + q_cols
        side_cols = -(-(2 * n_experts + 4) // LANES) * LANES
        gate_cols = -(-2 * n_experts // LANES) * LANES
        me_i, me_t = lax.axis_index("i"), lax.axis_index("t")

        side = jnp.concatenate(
            [
                w_router,
                norm1[:, None],
                norm2[:, None],
                jnp.zeros((depth, side_cols - n_experts - 2), bf16),
            ],
            axis=1,
        )
        pack = jnp.concatenate([w_query, w_key, w_value, w_out.T, side], axis=1)
        packed = lax.all_gather(pack, dp, axis=0, tiled=True)
        tokens_all = gather_t(tokens)

        def expert_piece(target):
            first = target * own_experts
            gate, up = (
                jnp.swapaxes(lax.dynamic_slice_in_dim(w, first, own_experts, 0), 0, 1)
                for w in (w_gate, w_up)
            )
            down = lax.dynamic_slice_in_dim(w_down, first, own_experts, 0).transpose(2, 0, 1)
            gate_up = jnp.concatenate(
                [gate.reshape(depth, own_hidden), up.reshape(depth, own_hidden)], axis=1
            )
            return gate_up, down.reshape(depth, own_hidden)

        def to_owner(piece, shift):
            pairs = [(m, (m + shift) % inner) for m in range(inner)]
            return jax.tree.map(lambda part: lax.ppermute(part, "i", pairs), piece)

        pieces = [expert_piece((me_i + shift) % inner) for shift in range(inner)]
        pieces, packed = tie(pieces, packed)
        tokens_all = tokens_all.astype(f32)
        far_down = to_owner(pieces[2][1], 2)
        near = to_owner(pieces[1], 1)
        owned = [pass_on(pieces[0])]

        w_qkv = packed[:, :qkv_cols]
        w_out_t = packed[:, qkv_cols:attn_cols]
        router = packed[:, attn_cols : attn_cols + n_experts]
        gains = packed[:, attn_cols + n_experts : attn_cols + n_experts + 2].astype(f32).T
        gain_one, gain_two = gains[0], gains[1]

        normal_all = tokens_all * rms_scale(tokens_all)
        normed_one = (normal_all * gain_one).astype(bf16)
        cosine, sine = rotary_tables(group, HEAD_DIM // 2)
        qkv = jnp.dot(normed_one, w_qkv, preferred_element_type=f32)
        query = rotate(qkv[:, :q_cols].reshape(group, -1, HEAD_DIM), cosine, sine).astype(bf16)
        keys = rotate(
            qkv[:, q_cols : q_cols + k_cols].reshape(group, -1, HEAD_DIM), cosine, sine
        ).astype(bf16)
        values = qkv[:, q_cols + k_cols :].astype(bf16).reshape(group, -1, HEAD_DIM)
        query, keys, values, far_down = tie(query, keys, values, far_down)
        attended, log_total = attend_forward(query, keys, values, prefix[0])
        far_piece, near, owned[0], attended = tie(pieces[2][0], near, owned[0], attended)
        far_gate_up = to_owner(far_piece, 2)
        branch = lax.dot_general(
            attended, w_out_t, (((1,), (1,)), ((), ())), preferred_element_type=f32
        ).astype(bf16)
        tokens_f = tokens.astype(f32)
        branch = scatter_t(branch)
        middle = tokens_f + branch
        scale_two = rms_scale(middle)
        normed_two = (middle * scale_two * gain_two).astype(bf16)

        logits = jnp.dot(normed_two, router, preferred_element_type=f32)
        own_routes = lax.dynamic_slice_in_dim(routes, me_t * rows, rows, 0)
        expert_ids = jnp.arange(n_experts, dtype=jnp.int32)
        routed = jnp.any(own_routes[:, :, None] == expert_ids[None, None, :], axis=1)
        gates = jnp.where(routed, jax.nn.softmax(jnp.where(routed, logits, -1e30), axis=-1), 0.0)
        gates_high = gates.astype(bf16)
        gates_low = (gates - gates_high.astype(f32)).astype(bf16)
        shipped = jnp.concatenate(
            [
                to_owner_order(normed_two),
                gates_high,
                gates_low,
                jnp.zeros((rows, gate_cols - 2 * n_experts), bf16),
            ],
            axis=1,
        )
        last, near, far_gate_up, shipped = tie(pieces[3], near, far_gate_up, shipped)
        last = to_owner(last, 3)
        owned += [pass_on(near), pass_on((far_gate_up, far_down)), pass_on(last)]
        shared_all = by_rows(lax.all_gather(by_rows(shipped), shared, axis=0, tiled=True))
        w_gate_up = jnp.zeros((outer, inner, depth, 2 * own_hidden), bf16)
        w_down_t = jnp.zeros((outer, inner, depth, own_hidden), bf16)
        for shift in range(inner):
            source = (me_i - shift) % inner
            w_gate_up = put(w_gate_up, owned[shift][0][:, None], 0, source, 0, 0)
            w_down_t = put(w_down_t, owned[shift][1][:, None], 0, source, 0, 0)
        cot_order, shared_all, w_gate_up, w_down_t = tie(
            by_rows(to_owner_order(cotangent)),
            shared_all,
            w_gate_up.reshape(outer * inner * depth, 2 * own_hidden),
            w_down_t.reshape(outer * inner * depth, own_hidden),
        )
        cot_all = by_rows(lax.all_gather(cot_order, shared, axis=0, tiled=True))
        count = shared_all.shape[0]
        normed_all = shared_all[:, :width]

        slot = jnp.arange(gate_cols, dtype=jnp.int32)[:, None]
        owner = me_i * own_experts + jnp.arange(own_hidden, dtype=jnp.int32)[None, :] // hidden
        spread = ((slot == owner) | (slot == owner + n_experts)).astype(bf16)
        gate_wide = jnp.dot(shared_all[:, width:], spread, preferred_element_type=f32)
        gate_up = jnp.dot(normed_all, w_gate_up, preferred_element_type=f32).astype(bf16)
        gate_up, gate_wide = tie(gate_up, gate_wide.astype(bf16))

        def activate(gate_up):
            gate_part = gate_up[:, :own_hidden].astype(f32)
            up_part = gate_up[:, own_hidden:].astype(f32)
            sigmoid_g = jax.nn.sigmoid(gate_part)
            return gate_part, up_part, sigmoid_g, gate_part * sigmoid_g

        _, up_part, _, silu_g = activate(gate_up)
        gated = (silu_g * up_part * gate_wide.astype(f32)).astype(bf16)
        expert_part = lax.dot_general(
            gated, w_down_t, (((1,), (1,)), ((), ())), preferred_element_type=f32
        ).astype(bf16)
        expert_part, cot_all, gate_up, gate_wide = tie(
            by_rows(expert_part), cot_all, gate_up, gate_wide
        )
        expert_share = lax.psum_scatter(expert_part, shared, scatter_dimension=0, tiled=True)
        contract_rows = (((0,), (0,)), ((), ()))
        grad_w_down = lax.dot_general(
            cot_all, gated, contract_rows, preferred_element_type=f32
        ).astype(bf16)
        grad_w_down, cot_all = tie(grad_w_down, cot_all)

        def to_sum(grad):
            by_owner = grad.reshape(outer, inner, depth, -1)
            return [
                sum_outer(
                    lax.dynamic_index_in_dim(by_owner, (me_i + shift) % inner, 1, keepdims=False)
                )
                for shift in range(inner)
            ]

        down_sums = to_sum(grad_w_down)
        cot_part = jnp.dot(cot_all, w_down_t, preferred_element_type=f32)
        gate_part, up_part, sigmoid_g, silu_g = activate(gate_up)
        grad_act = cot_part * gate_wide.astype(f32)
        grad_gate_up = jnp.concatenate(
            [
                (grad_act * up_part * sigmoid_g * (1.0 + gate_part * (1.0 - sigmoid_g))).astype(
                    bf16
                ),
                (grad_act * silu_g).astype(bf16),
            ],
            axis=1,
        )
        chosen = (jnp.arange(side_cols, dtype=jnp.int32)[None, :] == owner.T).astype(bf16)
        gate_block = jnp.dot(
            (silu_g * up_part * cot_part).astype(bf16), chosen, preferred_element_type=f32
        )
        grad_normed_part = lax.dot_general(
            grad_gate_up, w_gate_up, (((1,), (1,)), ((), ())), preferred_element_type=f32
        )
        grad_shipped = jnp.concatenate([grad_normed_part, gate_block], axis=1).astype(bf16)
        grad_shipped, down_sums, expert_share = tie(by_rows(grad_shipped), down_sums, expert_share)
        grad_back = lax.psum_scatter(grad_shipped, shared, scatter_dimension=0, tiled=True)
        shared_rows, _ = tie(shared_all, grad_shipped)
        grad_w_gate_up = lax.dot_general(
            shared_rows[:, :width], grad_gate_up, contract_rows, preferred_element_type=f32
        ).astype(bf16)
        gate_up_sums = to_sum(grad_w_gate_up)
        sent_down = down_sums[:1] + [to_owner(down_sums[s], s) for s in range(1, inner)]
        gate_up_sums, sent_down, grad_back = tie(gate_up_sums, sent_down, grad_back)
        sent_gate_up = gate_up_sums[:1] + [to_owner(gate_up_sums[s], s) for s in range(1, inner)]
        mixed = (middle + from_owner_order(expert_share).astype(f32)).astype(bf16)

        grad_back = grad_back.astype(f32)
        grad_chosen = grad_back[:, width : width + n_experts]
        grad_logits = gates * (
            grad_chosen - jnp.sum(gates * grad_chosen, axis=-1, keepdims=True)
        )
        grad_normed_two = from_owner_order(grad_back[:, :width]) + jnp.dot(
            grad_logits, router.astype(f32).T, precision=HIGHEST
        )
        grad_middle_part, normal_two = norm_backward(
            middle, scale_two, gain_two, grad_normed_two
        )
        grad_middle = cotangent.astype(f32) + grad_middle_part
        grad_gain_two = jnp.sum(grad_normed_two * normal_two, axis=0)
        grad_router_part = lax.dot_general(
            normed_two.astype(f32), grad_logits, contract_rows, precision=HIGHEST
        )
        grad_branch = gather_t(grad_middle.astype(bf16))
        grad_out_part = lax.dot_general(
            grad_branch, attended, contract_rows, preferred_element_type=f32
        ).astype(bf16)
        grad_out_part, sent_gate_up[2], grad_branch = tie(
            grad_out_part, sent_gate_up[2], grad_branch
        )
        grad_attended = jnp.dot(
            grad_branch, w_out_t, preferred_element_type=f32
        ).astype(bf16)
        sent_near = (sent_gate_up[1], sent_gate_up[3])
        grad_query, grad_keys, grad_values, sent_near = attend_backward(
            query, keys, values, grad_attended, log_total, prefix[0], sent_near
        )
        sent_gate_up[1], sent_gate_up[3] = sent_near
        grad_qkv = jnp.concatenate(
            [
                rotate(grad_query, cosine, -sine).astype(bf16).reshape(group, -1),
                rotate(grad_keys, cosine, -sine).astype(bf16).reshape(group, -1),
                grad_values.astype(bf16).reshape(group, -1),
            ],
            axis=1,
        )
        grad_normed_one = lax.dot_general(
            grad_qkv, w_qkv, (((1,), (1,)), ((), ())), preferred_element_type=f32
        )
        grad_gain_one = jnp.sum(grad_normed_one * normal_all, axis=0)
        own_grad_one = scatter_t(grad_normed_one.astype(bf16))
        sums = jnp.concatenate(
            [grad_router_part, grad_gain_one[:, None], grad_gain_two[:, None]], axis=1
        )
        (sums,) = tie(
            jnp.concatenate(
                [*split(sums), jnp.zeros((width, side_cols - 2 * n_experts - 4), bf16)], axis=1
            )
        )
        grad_attn = jnp.concatenate(
            [
                lax.dot_general(
                    normed_one, grad_qkv, contract_rows, preferred_element_type=f32
                ).astype(bf16),
                grad_out_part,
                sums,
            ],
            axis=1,
        )
        shard_attn = lax.psum_scatter(by_rows(grad_attn), dp, scatter_dimension=0, tiled=True)
        shard_attn, own_grad_one = tie(shard_attn, own_grad_one)
        shard_attn = shard_attn.astype(f32)
        grad_input_part, _ = norm_backward(tokens_f, rms_scale(tokens_f), gain_one, own_grad_one)
        grad_tokens = grad_middle + grad_input_part
        side_sum = shard_attn[:, attn_cols : attn_cols + 2 * n_experts + 4]
        side_sum = sum_tensor(jnp.sum(side_sum.reshape(depth, 2, -1), axis=1).T)

        grad_gate = jnp.zeros((n_experts, depth, hidden), f32)
        grad_up, grad_down = grad_gate, jnp.zeros((n_experts, hidden, depth), f32)
        for shift in range(inner):
            start = (me_i - shift) % inner * own_experts
            part = sent_down[shift]
            part = part.reshape(depth, own_experts, hidden).transpose(1, 2, 0)
            grad_down = put(grad_down, part.astype(f32), start, 0, 0)
            part = sent_gate_up[shift]
            part = part.reshape(depth, 2, own_experts, hidden).transpose(1, 2, 0, 3).astype(f32)
            grad_gate = put(grad_gate, part[0], start, 0, 0)
            grad_up = put(grad_up, part[1], start, 0, 0)
        return (
            mixed,
            grad_tokens,
            side_sum[n_experts],
            shard_attn[:, :q_cols],
            shard_attn[:, q_cols : q_cols + k_cols],
            shard_attn[:, q_cols + k_cols : qkv_cols],
            shard_attn[:, qkv_cols:attn_cols].T,
            side_sum[n_experts + 1],
            side_sum[:n_experts].T,
            grad_gate,
            grad_up,
            grad_down,
        )

    in_specs = (
        P(("i", "o", "t"), None),
        P(("i", "o", "t"), None),
        P(dp),
        P(dp, None),
        P(dp),
        P(dp, "t"),
        P(dp, "t"),
        P(dp, "t"),
        P("t", dp),
        P(dp),
        P(dp, None),
        P(None, dp, "t"),
        P(None, dp, "t"),
        P(None, "t", dp),
    )
    out_specs = (
        P(("i", "o", "t"), None),
        P(("i", "o", "t"), None),
        P(dp),
        P(dp, "t"),
        P(dp, "t"),
        P(dp, "t"),
        P("t", dp),
        P(dp),
        P(dp, None),
        P(None, dp, "t"),
        P(None, dp, "t"),
        P(None, "t", dp),
    )
    return jax.shard_map(
        on_device, mesh=grid, in_specs=in_specs, out_specs=out_specs, check_vma=False
    )
```

```python
import jax
import jax.numpy as jnp
from jax import lax
from jax.experimental.layout import Layout, with_layout_constraint
from jax.sharding import Mesh, PartitionSpec as P

HEAD_DIM = 64
EPSILON = 1e-05
LANES = 128
HIGHEST = lax.Precision.HIGHEST
f32 = jnp.float32
bf16 = jnp.bfloat16


def rms_scale(values):
    return lax.rsqrt(jnp.mean(values * values, axis=-1, keepdims=True) + EPSILON)


def norm_backward(values, scale, gain, grad_normed):
    normal_x = values * scale
    grad_hat = grad_normed * gain
    grad_values = scale * (
        grad_hat - normal_x * jnp.mean(grad_hat * normal_x, axis=-1, keepdims=True)
    )
    return grad_values, normal_x


def rotary_tables(row_count, half):
    position = jnp.arange(row_count, dtype=jnp.int32).astype(f32)
    inverse = jnp.power(10000.0, -jnp.arange(half, dtype=jnp.int32).astype(f32) / half)
    angle = position[:, None] * inverse[None, :]
    return jnp.cos(angle)[:, None, :], jnp.sin(angle)[:, None, :]


def rotate(tensor, cosine, sine):
    half = tensor.shape[-1] // 2
    first = tensor[..., :half]
    second = tensor[..., half:]
    return jnp.concatenate(
        [first * cosine - second * sine, second * cosine + first * sine], axis=-1
    )


def tie(*values):
    return lax.optimization_barrier(values)


def masked_scores(query, keys, prefix_len):
    seq_len, heads_kv, head_size = keys.shape
    grouped = query.reshape(seq_len, heads_kv, -1, head_size)
    scores = jnp.einsum(
        "qhgd,khd->hgqk", grouped, keys, preferred_element_type=f32
    ) * head_size ** (-0.5)
    row_ids = jnp.arange(seq_len, dtype=jnp.int32)
    allowed = (row_ids[None, :] <= row_ids[:, None]) | (row_ids[None, :] < prefix_len)
    return jnp.where(allowed, scores, -1e30), grouped


def attend_forward(query, keys, values, prefix_len):
    scores, _ = masked_scores(query, keys, prefix_len)
    highest = jnp.max(scores, axis=-1, keepdims=True)
    shifted = jnp.exp(scores - highest)
    summed = jnp.sum(shifted, axis=-1, keepdims=True)
    weights = (shifted / summed).astype(bf16)
    output = jnp.einsum("hgqk,khd->qhgd", weights, values, preferred_element_type=f32)
    return output.reshape(query.shape[0], -1).astype(bf16), highest + jnp.log(summed)


def attend_backward(query, keys, values, grad_mixed, log_total, prefix_len, hold):
    scores, grouped = masked_scores(query, keys, prefix_len)
    weights = jnp.exp(scores - log_total)
    seq_len, heads_kv, head_size = keys.shape
    grad_grouped = grad_mixed.reshape(seq_len, heads_kv, -1, head_size)
    grad_weights = jnp.einsum(
        "qhgd,khd->hgqk", grad_grouped, values, preferred_element_type=f32
    )
    grad_scores = (
        weights * (grad_weights - jnp.sum(weights * grad_weights, axis=-1, keepdims=True))
    ).astype(bf16)
    grad_scores, hold = tie(grad_scores, hold)
    scaling = head_size ** (-0.5)
    grad_query = (
        jnp.einsum("hgqk,khd->qhgd", grad_scores, keys, preferred_element_type=f32) * scaling
    )
    grad_keys = (
        jnp.einsum("hgqk,qhgd->khd", grad_scores, grouped, preferred_element_type=f32) * scaling
    )
    grad_values = jnp.einsum(
        "hgqk,qhgd->khd", weights.astype(bf16), grad_grouped, preferred_element_type=f32
    )
    return grad_query.reshape(seq_len, -1, head_size), grad_keys, grad_values, hold


def swap(values, axis, size, bit):
    return lax.ppermute(values, axis, [(m, m ^ bit) for m in range(size)])


def by_rows(values):
    return with_layout_constraint(values, Layout(major_to_minor=(0, 1)))


def split(values):
    high = values.astype(bf16)
    return high, (values - high.astype(f32)).astype(bf16)


def put(result, piece, *starts):
    return lax.dynamic_update_slice(result, piece, starts)


def solution(mesh):
    n_dp, n_tensor = mesh.shape["dp"], mesh.shape["tensor"]
    inner = 4
    outer = n_dp // inner
    grid = Mesh(mesh.devices.reshape(inner, outer, n_tensor), ("i", "o", "t"))
    dp = ("i", "o")
    shared = ("i", "t")

    def to_owner_order(values):
        rows = values.shape[0]
        if outer == 1:
            return values
        split = jnp.swapaxes(values.reshape(rows, inner, outer, -1), 1, 2)
        if outer == 2:
            split = jnp.where(lax.axis_index("o") == 0, split, split[:, ::-1])
        return split.reshape(rows, -1)

    def from_owner_order(values):
        rows = values.shape[0]
        if outer == 1:
            return values
        split = values.reshape(rows, outer, inner, -1)
        if outer == 2:
            split = jnp.where(lax.axis_index("o") == 0, split, split[:, ::-1])
        return jnp.swapaxes(split, 1, 2).reshape(rows, -1)

    def pass_on(pair):
        if outer == 2:
            return tuple(jnp.stack([piece, swap(piece, "o", 2, 1)]) for piece in pair)
        return tuple(lax.all_gather(piece, "o", axis=0) for piece in pair)

    def sum_outer(parts):
        if outer == 1:
            return parts[0]
        if outer == 2:
            return (parts[0].astype(f32) + swap(parts[1], "o", 2, 1).astype(f32)).astype(bf16)
        return lax.psum_scatter(parts, "o", scatter_dimension=0, tiled=False)

    def gather_t(block, hold=()):
        if n_tensor != 4:
            return tie(lax.all_gather(block, "t", axis=0, tiled=True), hold)
        rows, width = block.shape
        me_t = lax.axis_index("t")
        result = jnp.zeros((n_tensor * rows, width), block.dtype)
        pair = jnp.concatenate([block, swap(block, "t", n_tensor, 2)], axis=0)
        pair, hold = tie(pair, hold)
        for bit, part in ((0, pair), (1, swap(pair, "t", n_tensor, 1))):
            result = put(result, part[:rows], (me_t ^ bit) * rows, 0)
            result = put(result, part[rows:], (me_t ^ bit ^ 2) * rows, 0)
        return result, hold

    def scatter_t(values):
        if n_tensor != 4:
            return lax.psum_scatter(values, "t", scatter_dimension=0, tiled=True).astype(f32)
        me_t = lax.axis_index("t")
        block = values.reshape(2, 2, -1, values.shape[1])
        for axis, bit, own in ((1, 1, me_t % 2), (0, 2, me_t // 2)):
            keep = lax.dynamic_index_in_dim(block, own, axis, keepdims=False)
            send = lax.dynamic_index_in_dim(block, 1 - own, axis, keepdims=False)
            block = keep.astype(f32) + swap(send.astype(bf16), "t", n_tensor, bit).astype(f32)
        return block

    def sum_tensor(values):
        me_t = lax.axis_index("t")
        slots = put(jnp.zeros((n_tensor, *values.shape), f32), values[None], me_t, 0, 0)
        for shift in range(1, n_tensor):
            got = lax.ppermute(values, "t", [(m, (m + shift) % n_tensor) for m in range(n_tensor)])
            slots = put(slots, got[None], (me_t - shift) % n_tensor, 0, 0)
        return jnp.sum(slots, axis=0)

    def on_device(
        tokens,
        cotangent,
        prefix,
        routes,
        norm1,
        w_query,
        w_key,
        w_value,
        w_out,
        norm2,
        w_router,
        w_gate,
        w_up,
        w_down,
    ):
        rows, width = tokens.shape
        group = routes.shape[0]
        n_experts, depth, hidden = w_gate.shape
        own_experts = n_experts // inner
        own_hidden = own_experts * hidden
        q_cols, k_cols = w_query.shape[1], w_key.shape[1]
        qkv_cols = q_cols + 2 * k_cols
        attn_cols = qkv_cols + q_cols
        side_cols = -(-(2 * n_experts + 4) // LANES) * LANES
        gate_cols = -(-2 * n_experts // LANES) * LANES
        me_i, me_t = lax.axis_index("i"), lax.axis_index("t")

        side = jnp.concatenate(
            [
                w_router,
                norm1[:, None],
                norm2[:, None],
                jnp.zeros((depth, side_cols - n_experts - 2), bf16),
            ],
            axis=1,
        )
        pack = jnp.concatenate([w_query, w_key, w_value, w_out.T, side], axis=1)
        packed = lax.all_gather(pack, dp, axis=0, tiled=True)
        tokens_all, _ = gather_t(tokens)

        def expert_piece(target):
            first = target * own_experts
            gate, up = (
                jnp.swapaxes(lax.dynamic_slice_in_dim(w, first, own_experts, 0), 0, 1)
                for w in (w_gate, w_up)
            )
            down = lax.dynamic_slice_in_dim(w_down, first, own_experts, 0).transpose(2, 0, 1)
            gate_up = jnp.concatenate(
                [gate.reshape(depth, own_hidden), up.reshape(depth, own_hidden)], axis=1
            )
            return gate_up, down.reshape(depth, own_hidden)

        def to_owner(piece, shift):
            pairs = [(m, (m + shift) % inner) for m in range(inner)]
            return jax.tree.map(lambda part: lax.ppermute(part, "i", pairs), piece)

        pieces = [expert_piece((me_i + shift) % inner) for shift in range(inner)]
        pieces, packed = tie(pieces, packed)
        tokens_all = tokens_all.astype(f32)
        far_gate_up = to_owner(pieces[2][0], 2)
        owned = [pass_on(pieces[0])]

        w_qkv = packed[:, :qkv_cols]
        w_out_t = packed[:, qkv_cols:attn_cols]
        router = packed[:, attn_cols : attn_cols + n_experts]
        gains = packed[:, attn_cols + n_experts : attn_cols + n_experts + 2].astype(f32).T
        gain_one, gain_two = gains[0], gains[1]

        normal_all = tokens_all * rms_scale(tokens_all)
        normed_one = (normal_all * gain_one).astype(bf16)
        cosine, sine = rotary_tables(group, HEAD_DIM // 2)
        qkv = jnp.dot(normed_one, w_qkv, preferred_element_type=f32)
        query = rotate(qkv[:, :q_cols].reshape(group, -1, HEAD_DIM), cosine, sine).astype(bf16)
        keys = rotate(
            qkv[:, q_cols : q_cols + k_cols].reshape(group, -1, HEAD_DIM), cosine, sine
        ).astype(bf16)
        values = qkv[:, q_cols + k_cols :].astype(bf16).reshape(group, -1, HEAD_DIM)
        attended, log_total = attend_forward(query, keys, values, prefix[0])
        far_down, near, far_gate_up, owned[0], attended = tie(
            pieces[2][1], pieces[1], far_gate_up, owned[0], attended
        )
        far_down, near = to_owner(far_down, 2), to_owner(near, 1)
        branch = lax.dot_general(
            attended, w_out_t, (((1,), (1,)), ((), ())), preferred_element_type=f32
        ).astype(bf16)
        tokens_f = tokens.astype(f32)
        branch, far_down = tie(scatter_t(branch), far_down)
        middle = tokens_f + branch
        scale_two = rms_scale(middle)
        normed_two = (middle * scale_two * gain_two).astype(bf16)

        logits = jnp.dot(normed_two, router, preferred_element_type=f32)
        own_routes = lax.dynamic_slice_in_dim(routes, me_t * rows, rows, 0)
        expert_ids = jnp.arange(n_experts, dtype=jnp.int32)
        routed = jnp.any(own_routes[:, :, None] == expert_ids[None, None, :], axis=1)
        gates = jnp.where(routed, jax.nn.softmax(jnp.where(routed, logits, -1e30), axis=-1), 0.0)
        gates_high = gates.astype(bf16)
        gates_low = (gates - gates_high.astype(f32)).astype(bf16)
        shipped = jnp.concatenate(
            [
                to_owner_order(normed_two),
                gates_high,
                gates_low,
                jnp.zeros((rows, gate_cols - 2 * n_experts), bf16),
            ],
            axis=1,
        )
        last, near, shipped = tie(pieces[3], near, shipped)
        last = to_owner(last, 3)
        owned += [pass_on(near), pass_on((far_gate_up, far_down)), pass_on(last)]
        shared_all = by_rows(lax.all_gather(by_rows(shipped), shared, axis=0, tiled=True))
        w_gate_up = jnp.zeros((outer, inner, depth, 2 * own_hidden), bf16)
        w_down_t = jnp.zeros((outer, inner, depth, own_hidden), bf16)
        for shift in range(inner):
            source = (me_i - shift) % inner
            w_gate_up = put(w_gate_up, owned[shift][0][:, None], 0, source, 0, 0)
            w_down_t = put(w_down_t, owned[shift][1][:, None], 0, source, 0, 0)
        cot_order, shared_all, w_gate_up, w_down_t = tie(
            by_rows(to_owner_order(cotangent)),
            shared_all,
            w_gate_up.reshape(outer * inner * depth, 2 * own_hidden),
            w_down_t.reshape(outer * inner * depth, own_hidden),
        )
        cot_all = by_rows(lax.all_gather(cot_order, shared, axis=0, tiled=True))
        count = shared_all.shape[0]
        normed_all = shared_all[:, :width]

        slot = jnp.arange(gate_cols, dtype=jnp.int32)[:, None]
        owner = me_i * own_experts + jnp.arange(own_hidden, dtype=jnp.int32)[None, :] // hidden
        spread = ((slot == owner) | (slot == owner + n_experts)).astype(bf16)
        gate_wide = jnp.dot(shared_all[:, width:], spread, preferred_element_type=f32)
        gate_up = jnp.dot(normed_all, w_gate_up, preferred_element_type=f32).astype(bf16)
        gate_up, gate_wide = tie(gate_up, gate_wide.astype(bf16))

        def activate(gate_up):
            gate_part = gate_up[:, :own_hidden].astype(f32)
            up_part = gate_up[:, own_hidden:].astype(f32)
            sigmoid_g = jax.nn.sigmoid(gate_part)
            return gate_part, up_part, sigmoid_g, gate_part * sigmoid_g

        _, up_part, _, silu_g = activate(gate_up)
        gated = (silu_g * up_part * gate_wide.astype(f32)).astype(bf16)
        expert_part = lax.dot_general(
            gated, w_down_t, (((1,), (1,)), ((), ())), preferred_element_type=f32
        ).astype(bf16)
        expert_part, cot_all, gate_up, gate_wide = tie(
            by_rows(expert_part), cot_all, gate_up, gate_wide
        )
        expert_share = lax.psum_scatter(expert_part, shared, scatter_dimension=0, tiled=True)
        contract_rows = (((0,), (0,)), ((), ()))
        grad_w_down = lax.dot_general(
            cot_all, gated, contract_rows, preferred_element_type=f32
        ).astype(bf16)
        grad_w_down, cot_all = tie(grad_w_down, cot_all)

        def to_sum(grad):
            by_owner = grad.reshape(outer, inner, depth, -1)
            return [
                sum_outer(
                    lax.dynamic_index_in_dim(by_owner, (me_i + shift) % inner, 1, keepdims=False)
                )
                for shift in range(inner)
            ]

        down_sums = to_sum(grad_w_down)
        cot_part = jnp.dot(cot_all, w_down_t, preferred_element_type=f32)
        gate_part, up_part, sigmoid_g, silu_g = activate(gate_up)
        grad_act = cot_part * gate_wide.astype(f32)
        grad_gate_up = jnp.concatenate(
            [
                (grad_act * up_part * sigmoid_g * (1.0 + gate_part * (1.0 - sigmoid_g))).astype(
                    bf16
                ),
                (grad_act * silu_g).astype(bf16),
            ],
            axis=1,
        )
        products, grad_gate_up, down_sums = tie(
            (silu_g * up_part * cot_part).astype(bf16), grad_gate_up, down_sums
        )
        sent_down = down_sums[:1] + [to_owner(down_sums[s], s) for s in range(1, inner)]
        chosen = (jnp.arange(side_cols, dtype=jnp.int32)[None, :] == owner.T).astype(bf16)
        gate_block = jnp.dot(products, chosen, preferred_element_type=f32)
        grad_normed_part = lax.dot_general(
            grad_gate_up, w_gate_up, (((1,), (1,)), ((), ())), preferred_element_type=f32
        )
        grad_shipped = jnp.concatenate([grad_normed_part, gate_block], axis=1).astype(bf16)
        grad_shipped, sent_down, expert_share = tie(by_rows(grad_shipped), sent_down, expert_share)
        grad_back = lax.psum_scatter(grad_shipped, shared, scatter_dimension=0, tiled=True)
        shared_rows, _ = tie(shared_all, grad_shipped)
        grad_w_gate_up = lax.dot_general(
            shared_rows[:, :width], grad_gate_up, contract_rows, preferred_element_type=f32
        ).astype(bf16)
        gate_up_sums = to_sum(grad_w_gate_up)
        grad_down = jnp.zeros((n_experts, hidden, depth), f32)
        for shift in range(inner):
            part = sent_down[shift].reshape(depth, own_experts, hidden).transpose(1, 2, 0)
            grad_down = put(
                grad_down, part.astype(f32), (me_i - shift) % inner * own_experts, 0, 0
            )
        gate_up_sums, grad_down, grad_back = tie(gate_up_sums, grad_down, grad_back)
        far_sum_gate, far_sum_up = jnp.split(gate_up_sums[2], 2, axis=1)
        sent_gate_up = {0: jnp.split(gate_up_sums[0], 2, axis=1)}
        mixed = (middle + from_owner_order(expert_share).astype(f32)).astype(bf16)

        grad_back = grad_back.astype(f32)
        grad_chosen = grad_back[:, width : width + n_experts]
        grad_logits = gates * (
            grad_chosen - jnp.sum(gates * grad_chosen, axis=-1, keepdims=True)
        )
        grad_normed_two = from_owner_order(grad_back[:, :width]) + jnp.dot(
            grad_logits, router.astype(f32).T, precision=HIGHEST
        )
        grad_middle_part, normal_two = norm_backward(
            middle, scale_two, gain_two, grad_normed_two
        )
        grad_middle = cotangent.astype(f32) + grad_middle_part
        grad_gain_two = jnp.sum(grad_normed_two * normal_two, axis=0)
        grad_router_part = lax.dot_general(
            normed_two.astype(f32), grad_logits, contract_rows, precision=HIGHEST
        )
        sent_gate = to_owner(far_sum_gate, 2)
        grad_branch, (sent_gate, far_sum_up) = gather_t(
            grad_middle.astype(bf16), (sent_gate, far_sum_up)
        )
        sent_up = to_owner(far_sum_up, 2)
        grad_out_part = lax.dot_general(
            grad_branch, attended, contract_rows, preferred_element_type=f32
        ).astype(bf16)
        grad_out_part, grad_branch, near_sum, sent_up = tie(
            grad_out_part, grad_branch, gate_up_sums[1], sent_up
        )
        sent_gate_up[2] = (sent_gate, sent_up)
        sent_gate_up[1] = to_owner(near_sum, 1)
        grad_attended = jnp.dot(
            grad_branch, w_out_t, preferred_element_type=f32
        ).astype(bf16)
        grad_query, grad_keys, grad_values, (sent_gate_up[1], last_sum) = attend_backward(
            query,
            keys,
            values,
            grad_attended,
            log_total,
            prefix[0],
            (sent_gate_up[1], gate_up_sums[3]),
        )
        sent_gate_up[3] = to_owner(last_sum, 3)
        grad_query, grad_keys, grad_values, sent_gate_up[3] = tie(
            grad_query, grad_keys, grad_values, sent_gate_up[3]
        )
        for shift in (1, 3):
            sent_gate_up[shift] = jnp.split(sent_gate_up[shift], 2, axis=1)
        grad_qkv = jnp.concatenate(
            [
                rotate(grad_query, cosine, -sine).astype(bf16).reshape(group, -1),
                rotate(grad_keys, cosine, -sine).astype(bf16).reshape(group, -1),
                grad_values.astype(bf16).reshape(group, -1),
            ],
            axis=1,
        )
        grad_normed_one = lax.dot_general(
            grad_qkv, w_qkv, (((1,), (1,)), ((), ())), preferred_element_type=f32
        )
        grad_gain_one = jnp.sum(grad_normed_one * normal_all, axis=0)
        own_grad_one = scatter_t(grad_normed_one.astype(bf16))
        sums = jnp.concatenate(
            [grad_router_part, grad_gain_one[:, None], grad_gain_two[:, None]], axis=1
        )
        (sums,) = tie(
            jnp.concatenate(
                [*split(sums), jnp.zeros((width, side_cols - 2 * n_experts - 4), bf16)], axis=1
            )
        )
        grad_attn = jnp.concatenate(
            [
                lax.dot_general(
                    normed_one, grad_qkv, contract_rows, preferred_element_type=f32
                ).astype(bf16),
                grad_out_part,
                sums,
            ],
            axis=1,
        )
        shard_attn = lax.psum_scatter(by_rows(grad_attn), dp, scatter_dimension=0, tiled=True)
        shard_attn = shard_attn.astype(f32)
        grad_input_part, _ = norm_backward(tokens_f, rms_scale(tokens_f), gain_one, own_grad_one)
        grad_tokens = grad_middle + grad_input_part
        side_sum = shard_attn[:, attn_cols : attn_cols + 2 * n_experts + 4]
        side_sum = sum_tensor(jnp.sum(side_sum.reshape(depth, 2, -1), axis=1).T)

        sent_gate_up[1], sent_gate_up[3], own_grad_one = tie(
            sent_gate_up[1], sent_gate_up[3], own_grad_one
        )
        grad_gate = jnp.zeros((n_experts, depth, hidden), f32)
        grad_up = grad_gate
        for shift in range(inner):
            start = (me_i - shift) % inner * own_experts
            gate, up = (
                jnp.swapaxes(part.reshape(depth, own_experts, hidden), 0, 1).astype(f32)
                for part in sent_gate_up[shift]
            )
            grad_gate = put(grad_gate, gate, start, 0, 0)
            grad_up = put(grad_up, up, start, 0, 0)
        return (
            mixed,
            grad_tokens,
            side_sum[n_experts],
            shard_attn[:, :q_cols],
            shard_attn[:, q_cols : q_cols + k_cols],
            shard_attn[:, q_cols + k_cols : qkv_cols],
            shard_attn[:, qkv_cols:attn_cols].T,
            side_sum[n_experts + 1],
            side_sum[:n_experts].T,
            grad_gate,
            grad_up,
            grad_down,
        )

    in_specs = (
        P(("i", "o", "t"), None),
        P(("i", "o", "t"), None),
        P(dp),
        P(dp, None),
        P(dp),
        P(dp, "t"),
        P(dp, "t"),
        P(dp, "t"),
        P("t", dp),
        P(dp),
        P(dp, None),
        P(None, dp, "t"),
        P(None, dp, "t"),
        P(None, "t", dp),
    )
    out_specs = (
        P(("i", "o", "t"), None),
        P(("i", "o", "t"), None),
        P(dp),
        P(dp, "t"),
        P(dp, "t"),
        P(dp, "t"),
        P("t", dp),
        P(dp),
        P(dp, None),
        P(None, dp, "t"),
        P(None, dp, "t"),
        P(None, "t", dp),
    )
    return jax.shard_map(
        on_device, mesh=grid, in_specs=in_specs, out_specs=out_specs, check_vma=False
    )
```

```python
import jax
import jax.numpy as jnp
from jax import lax
from jax.experimental.layout import Layout, with_layout_constraint
from jax.sharding import Mesh, PartitionSpec as P

HEAD_DIM = 64
EPSILON = 1e-05
LANES = 128
HIGHEST = lax.Precision.HIGHEST
f32 = jnp.float32
bf16 = jnp.bfloat16


def rms_scale(values):
    return lax.rsqrt(jnp.mean(values * values, axis=-1, keepdims=True) + EPSILON)


def norm_backward(values, scale, gain, grad_normed):
    normal_x = values * scale
    grad_hat = grad_normed * gain
    grad_values = scale * (
        grad_hat - normal_x * jnp.mean(grad_hat * normal_x, axis=-1, keepdims=True)
    )
    return grad_values, normal_x


def rotary_tables(row_count, half):
    position = jnp.arange(row_count, dtype=jnp.int32).astype(f32)
    inverse = jnp.power(10000.0, -jnp.arange(half, dtype=jnp.int32).astype(f32) / half)
    angle = position[:, None] * inverse[None, :]
    return jnp.cos(angle)[:, None, :], jnp.sin(angle)[:, None, :]


def rotate(tensor, cosine, sine):
    half = tensor.shape[-1] // 2
    first = tensor[..., :half]
    second = tensor[..., half:]
    return jnp.concatenate(
        [first * cosine - second * sine, second * cosine + first * sine], axis=-1
    )


def tie(*values):
    return lax.optimization_barrier(values)


def masked_scores(query, keys, prefix_len):
    seq_len, heads_kv, head_size = keys.shape
    grouped = query.reshape(seq_len, heads_kv, -1, head_size)
    scores = jnp.einsum(
        "qhgd,khd->hgqk", grouped, keys, preferred_element_type=f32
    ) * head_size ** (-0.5)
    row_ids = jnp.arange(seq_len, dtype=jnp.int32)
    allowed = (row_ids[None, :] <= row_ids[:, None]) | (row_ids[None, :] < prefix_len)
    return jnp.where(allowed, scores, -1e30), grouped


def attend_forward(query, keys, values, prefix_len):
    scores, _ = masked_scores(query, keys, prefix_len)
    highest = jnp.max(scores, axis=-1, keepdims=True)
    shifted = jnp.exp(scores - highest)
    summed = jnp.sum(shifted, axis=-1, keepdims=True)
    weights = (shifted / summed).astype(bf16)
    output = jnp.einsum("hgqk,khd->qhgd", weights, values, preferred_element_type=f32)
    return output.reshape(query.shape[0], -1).astype(bf16), highest + jnp.log(summed)


def attend_backward(query, keys, values, grad_mixed, log_total, prefix_len, hold):
    scores, grouped = masked_scores(query, keys, prefix_len)
    weights = jnp.exp(scores - log_total)
    seq_len, heads_kv, head_size = keys.shape
    grad_grouped = grad_mixed.reshape(seq_len, heads_kv, -1, head_size)
    grad_weights = jnp.einsum(
        "qhgd,khd->hgqk", grad_grouped, values, preferred_element_type=f32
    )
    grad_scores = (
        weights * (grad_weights - jnp.sum(weights * grad_weights, axis=-1, keepdims=True))
    ).astype(bf16)
    grad_scores, hold = tie(grad_scores, hold)
    scaling = head_size ** (-0.5)
    grad_query = (
        jnp.einsum("hgqk,khd->qhgd", grad_scores, keys, preferred_element_type=f32) * scaling
    )
    grad_keys = (
        jnp.einsum("hgqk,qhgd->khd", grad_scores, grouped, preferred_element_type=f32) * scaling
    )
    grad_values = jnp.einsum(
        "hgqk,qhgd->khd", weights.astype(bf16), grad_grouped, preferred_element_type=f32
    )
    return grad_query.reshape(seq_len, -1, head_size), grad_keys, grad_values, hold


def swap(values, axis, size, bit):
    return lax.ppermute(values, axis, [(m, m ^ bit) for m in range(size)])


def by_rows(values):
    return with_layout_constraint(values, Layout(major_to_minor=(0, 1)))


def split(values):
    high = values.astype(bf16)
    return high, (values - high.astype(f32)).astype(bf16)


def put(result, piece, *starts):
    return lax.dynamic_update_slice(result, piece, starts)


def solution(mesh):
    n_dp, n_tensor = mesh.shape["dp"], mesh.shape["tensor"]
    inner = 4
    outer = n_dp // inner
    grid = Mesh(mesh.devices.reshape(inner, outer, n_tensor), ("i", "o", "t"))
    dp = ("i", "o")
    shared = ("i", "t")

    def to_owner_order(values):
        rows = values.shape[0]
        if outer == 1:
            return values
        split = jnp.swapaxes(values.reshape(rows, inner, outer, -1), 1, 2)
        if outer == 2:
            split = jnp.where(lax.axis_index("o") == 0, split, split[:, ::-1])
        return split.reshape(rows, -1)

    def from_owner_order(values):
        rows = values.shape[0]
        if outer == 1:
            return values
        split = values.reshape(rows, outer, inner, -1)
        if outer == 2:
            split = jnp.where(lax.axis_index("o") == 0, split, split[:, ::-1])
        return jnp.swapaxes(split, 1, 2).reshape(rows, -1)

    def pass_on(pair):
        if outer == 2:
            return tuple(jnp.stack([piece, swap(piece, "o", 2, 1)]) for piece in pair)
        return tuple(lax.all_gather(piece, "o", axis=0) for piece in pair)

    def sum_outer(parts):
        if outer == 1:
            return parts[0]
        if outer == 2:
            return (parts[0].astype(f32) + swap(parts[1], "o", 2, 1).astype(f32)).astype(bf16)
        return lax.psum_scatter(parts, "o", scatter_dimension=0, tiled=False)

    def gather_t(block, hold=()):
        if n_tensor != 4:
            return tie(lax.all_gather(block, "t", axis=0, tiled=True), hold)
        rows, width = block.shape
        me_t = lax.axis_index("t")
        result = jnp.zeros((n_tensor * rows, width), block.dtype)
        pair = jnp.concatenate([block, swap(block, "t", n_tensor, 2)], axis=0)
        pair, hold = tie(pair, hold)
        for bit, part in ((0, pair), (1, swap(pair, "t", n_tensor, 1))):
            result = put(result, part[:rows], (me_t ^ bit) * rows, 0)
            result = put(result, part[rows:], (me_t ^ bit ^ 2) * rows, 0)
        return result, hold

    def scatter_t(values):
        if n_tensor != 4:
            return lax.psum_scatter(values, "t", scatter_dimension=0, tiled=True).astype(f32)
        me_t = lax.axis_index("t")
        block = values.reshape(2, 2, -1, values.shape[1])
        for axis, bit, own in ((1, 1, me_t % 2), (0, 2, me_t // 2)):
            keep = lax.dynamic_index_in_dim(block, own, axis, keepdims=False)
            send = lax.dynamic_index_in_dim(block, 1 - own, axis, keepdims=False)
            block = keep.astype(f32) + swap(send.astype(bf16), "t", n_tensor, bit).astype(f32)
        return block

    def sum_tensor(values):
        me_t = lax.axis_index("t")
        slots = put(jnp.zeros((n_tensor, *values.shape), f32), values[None], me_t, 0, 0)
        for shift in range(1, n_tensor):
            got = lax.ppermute(values, "t", [(m, (m + shift) % n_tensor) for m in range(n_tensor)])
            slots = put(slots, got[None], (me_t - shift) % n_tensor, 0, 0)
        return jnp.sum(slots, axis=0)

    def on_device(
        tokens,
        cotangent,
        prefix,
        routes,
        norm1,
        w_query,
        w_key,
        w_value,
        w_out,
        norm2,
        w_router,
        w_gate,
        w_up,
        w_down,
    ):
        rows, width = tokens.shape
        group = routes.shape[0]
        n_experts, depth, hidden = w_gate.shape
        own_experts = n_experts // inner
        own_hidden = own_experts * hidden
        q_cols, k_cols = w_query.shape[1], w_key.shape[1]
        qkv_cols = q_cols + 2 * k_cols
        attn_cols = qkv_cols + q_cols
        side_cols = -(-(2 * n_experts + 4) // LANES) * LANES
        gate_cols = -(-2 * n_experts // LANES) * LANES
        me_i, me_t = lax.axis_index("i"), lax.axis_index("t")

        side = jnp.concatenate(
            [
                w_router,
                norm1[:, None],
                norm2[:, None],
                jnp.zeros((depth, side_cols - n_experts - 2), bf16),
            ],
            axis=1,
        )
        pack = jnp.concatenate([w_query, w_key, w_value, w_out.T, side], axis=1)
        packed = lax.all_gather(pack, dp, axis=0, tiled=True)
        tokens_all, _ = gather_t(tokens)

        def expert_piece(target):
            first = target * own_experts
            gate, up = (
                jnp.swapaxes(lax.dynamic_slice_in_dim(w, first, own_experts, 0), 0, 1)
                for w in (w_gate, w_up)
            )
            down = lax.dynamic_slice_in_dim(w_down, first, own_experts, 0).transpose(2, 0, 1)
            gate_up = jnp.concatenate(
                [gate.reshape(depth, own_hidden), up.reshape(depth, own_hidden)], axis=1
            )
            return by_rows(gate_up), by_rows(down.reshape(depth, own_hidden))

        def to_owner(piece, shift):
            pairs = [(m, (m + shift) % inner) for m in range(inner)]
            return jax.tree.map(lambda part: lax.ppermute(part, "i", pairs), piece)

        pieces = [expert_piece((me_i + shift) % inner) for shift in range(inner)]
        pieces, packed = tie(pieces, packed)
        tokens_all = tokens_all.astype(f32)
        far_gate_up = to_owner(pieces[2][0], 2)
        owned = [pass_on(pieces[0])]

        w_qkv = packed[:, :qkv_cols]
        w_out_t = packed[:, qkv_cols:attn_cols]
        router = packed[:, attn_cols : attn_cols + n_experts]
        gains = packed[:, attn_cols + n_experts : attn_cols + n_experts + 2].astype(f32).T
        gain_one, gain_two = gains[0], gains[1]

        normal_all = tokens_all * rms_scale(tokens_all)
        normed_one = (normal_all * gain_one).astype(bf16)
        cosine, sine = rotary_tables(group, HEAD_DIM // 2)
        qkv = jnp.dot(normed_one, w_qkv, preferred_element_type=f32)
        query = rotate(qkv[:, :q_cols].reshape(group, -1, HEAD_DIM), cosine, sine).astype(bf16)
        keys = rotate(
            qkv[:, q_cols : q_cols + k_cols].reshape(group, -1, HEAD_DIM), cosine, sine
        ).astype(bf16)
        values = qkv[:, q_cols + k_cols :].astype(bf16).reshape(group, -1, HEAD_DIM)
        attended, log_total = attend_forward(query, keys, values, prefix[0])
        far_down, far_gate_up, owned[0], attended = tie(
            pieces[2][1], far_gate_up, owned[0], attended
        )
        far_down = to_owner(far_down, 2)
        branch = lax.dot_general(
            attended, w_out_t, (((1,), (1,)), ((), ())), preferred_element_type=f32
        ).astype(bf16)
        tokens_f = tokens.astype(f32)
        branch = scatter_t(branch)
        middle = tokens_f + branch
        scale_two = rms_scale(middle)
        normed_two = (middle * scale_two * gain_two).astype(bf16)

        logits = jnp.dot(normed_two, router, preferred_element_type=f32)
        own_routes = lax.dynamic_slice_in_dim(routes, me_t * rows, rows, 0)
        expert_ids = jnp.arange(n_experts, dtype=jnp.int32)
        routed = jnp.any(own_routes[:, :, None] == expert_ids[None, None, :], axis=1)
        gates = jnp.where(routed, jax.nn.softmax(jnp.where(routed, logits, -1e30), axis=-1), 0.0)
        gates_high = gates.astype(bf16)
        gates_low = (gates - gates_high.astype(f32)).astype(bf16)
        shipped = jnp.concatenate(
            [
                to_owner_order(normed_two),
                gates_high,
                gates_low,
                jnp.zeros((rows, gate_cols - 2 * n_experts), bf16),
            ],
            axis=1,
        )
        last, near, far_down, shipped = tie(pieces[3], pieces[1], far_down, shipped)
        last, near = to_owner(last, 3), to_owner(near, 1)
        owned += [pass_on(near), pass_on((far_gate_up, far_down)), pass_on(last)]
        shared_all = by_rows(lax.all_gather(by_rows(shipped), shared, axis=0, tiled=True))
        w_gate_up = jnp.zeros((outer, inner, depth, 2 * own_hidden), bf16)
        w_down_t = jnp.zeros((outer, inner, depth, own_hidden), bf16)
        for shift in range(inner):
            source = (me_i - shift) % inner
            w_gate_up = put(w_gate_up, owned[shift][0][:, None], 0, source, 0, 0)
            w_down_t = put(w_down_t, owned[shift][1][:, None], 0, source, 0, 0)
        cot_order, shared_all, w_gate_up, w_down_t = tie(
            by_rows(to_owner_order(cotangent)),
            shared_all,
            w_gate_up.reshape(outer * inner * depth, 2 * own_hidden),
            w_down_t.reshape(outer * inner * depth, own_hidden),
        )
        cot_all = by_rows(lax.all_gather(cot_order, shared, axis=0, tiled=True))
        count = shared_all.shape[0]
        normed_all = shared_all[:, :width]

        slot = jnp.arange(gate_cols, dtype=jnp.int32)[:, None]
        owner = me_i * own_experts + jnp.arange(own_hidden, dtype=jnp.int32)[None, :] // hidden
        spread = ((slot == owner) | (slot == owner + n_experts)).astype(bf16)
        gate_wide = jnp.dot(shared_all[:, width:], spread, preferred_element_type=f32)
        gate_up = jnp.dot(normed_all, w_gate_up, preferred_element_type=f32).astype(bf16)
        gate_up, gate_wide = tie(gate_up, gate_wide.astype(bf16))

        def activate(gate_up):
            gate_part = gate_up[:, :own_hidden].astype(f32)
            up_part = gate_up[:, own_hidden:].astype(f32)
            sigmoid_g = jax.nn.sigmoid(gate_part)
            return gate_part, up_part, sigmoid_g, gate_part * sigmoid_g

        _, up_part, _, silu_g = activate(gate_up)
        gated = (silu_g * up_part * gate_wide.astype(f32)).astype(bf16)
        expert_part = lax.dot_general(
            gated, w_down_t, (((1,), (1,)), ((), ())), preferred_element_type=f32
        ).astype(bf16)
        expert_part, cot_all, gate_up, gate_wide = tie(
            by_rows(expert_part), cot_all, gate_up, gate_wide
        )
        expert_share = lax.psum_scatter(expert_part, shared, scatter_dimension=0, tiled=True)
        contract_rows = (((0,), (0,)), ((), ()))
        grad_w_down = lax.dot_general(
            cot_all, gated, contract_rows, preferred_element_type=f32
        ).astype(bf16)
        grad_w_down, cot_all = tie(grad_w_down, cot_all)

        def to_sum(grad):
            by_owner = grad.reshape(outer, inner, depth, -1)
            return [
                sum_outer(
                    lax.dynamic_index_in_dim(by_owner, (me_i + shift) % inner, 1, keepdims=False)
                )
                for shift in range(inner)
            ]

        down_sums = to_sum(grad_w_down)
        cot_part = jnp.dot(cot_all, w_down_t, preferred_element_type=f32)
        gate_part, up_part, sigmoid_g, silu_g = activate(gate_up)
        grad_act = cot_part * gate_wide.astype(f32)
        grad_gate_up = jnp.concatenate(
            [
                (grad_act * up_part * sigmoid_g * (1.0 + gate_part * (1.0 - sigmoid_g))).astype(
                    bf16
                ),
                (grad_act * silu_g).astype(bf16),
            ],
            axis=1,
        )
        products, down_sums = tie((silu_g * up_part * cot_part).astype(bf16), down_sums)
        sent_down = down_sums[:1] + [to_owner(down_sums[s], s) for s in range(1, inner)]
        chosen = (jnp.arange(side_cols, dtype=jnp.int32)[None, :] == owner.T).astype(bf16)
        gate_block = jnp.dot(products, chosen, preferred_element_type=f32)
        grad_normed_part = lax.dot_general(
            grad_gate_up, w_gate_up, (((1,), (1,)), ((), ())), preferred_element_type=f32
        )
        grad_shipped = jnp.concatenate([grad_normed_part, gate_block], axis=1).astype(bf16)
        grad_shipped, sent_down, expert_share = tie(by_rows(grad_shipped), sent_down, expert_share)
        grad_back = lax.psum_scatter(grad_shipped, shared, scatter_dimension=0, tiled=True)
        shared_rows, _ = tie(shared_all, grad_shipped)
        grad_w_gate_up = lax.dot_general(
            shared_rows[:, :width], grad_gate_up, contract_rows, preferred_element_type=f32
        ).astype(bf16)
        gate_up_sums = to_sum(grad_w_gate_up)
        grad_down = jnp.zeros((n_experts, hidden, depth), f32)
        for shift in range(inner):
            part = sent_down[shift].reshape(depth, own_experts, hidden).transpose(1, 2, 0)
            grad_down = put(
                grad_down, part.astype(f32), (me_i - shift) % inner * own_experts, 0, 0
            )
        gate_up_sums, grad_down, grad_back = tie(gate_up_sums, grad_down, grad_back)
        far_sum_gate, far_sum_up = jnp.split(gate_up_sums[2], 2, axis=1)
        sent_gate_up = {0: jnp.split(gate_up_sums[0], 2, axis=1)}
        mixed = (middle + from_owner_order(expert_share).astype(f32)).astype(bf16)

        grad_back = grad_back.astype(f32)
        grad_chosen = grad_back[:, width : width + n_experts]
        grad_logits = gates * (
            grad_chosen - jnp.sum(gates * grad_chosen, axis=-1, keepdims=True)
        )
        grad_normed_two = from_owner_order(grad_back[:, :width]) + jnp.dot(
            grad_logits, router.astype(f32).T, precision=HIGHEST
        )
        grad_middle_part, normal_two = norm_backward(
            middle, scale_two, gain_two, grad_normed_two
        )
        grad_middle = cotangent.astype(f32) + grad_middle_part
        grad_gain_two = jnp.sum(grad_normed_two * normal_two, axis=0)
        grad_router_part = lax.dot_general(
            normed_two.astype(f32), grad_logits, contract_rows, precision=HIGHEST
        )
        sent_gate = to_owner(far_sum_gate, 2)
        grad_branch, (sent_gate, far_sum_up) = gather_t(
            grad_middle.astype(bf16), (sent_gate, far_sum_up)
        )
        sent_up = to_owner(far_sum_up, 2)
        grad_out_part = lax.dot_general(
            grad_branch, attended, contract_rows, preferred_element_type=f32
        ).astype(bf16)
        grad_out_part, grad_branch = tie(grad_out_part, grad_branch)
        grad_attended = jnp.dot(
            grad_branch, w_out_t, preferred_element_type=f32
        ).astype(bf16)
        grad_query, grad_keys, grad_values, (sent_up, near_sum, last_sum) = attend_backward(
            query,
            keys,
            values,
            grad_attended,
            log_total,
            prefix[0],
            (sent_up, gate_up_sums[1], gate_up_sums[3]),
        )
        sent_gate_up[2] = (sent_gate, sent_up)
        sent_gate_up[1], sent_gate_up[3] = to_owner(near_sum, 1), to_owner(last_sum, 3)
        grad_query, grad_keys, grad_values, sent_gate_up[1] = tie(
            grad_query, grad_keys, grad_values, sent_gate_up[1]
        )
        for shift in (1, 3):
            sent_gate_up[shift] = jnp.split(sent_gate_up[shift], 2, axis=1)
        grad_qkv = jnp.concatenate(
            [
                rotate(grad_query, cosine, -sine).astype(bf16).reshape(group, -1),
                rotate(grad_keys, cosine, -sine).astype(bf16).reshape(group, -1),
                grad_values.astype(bf16).reshape(group, -1),
            ],
            axis=1,
        )
        grad_normed_one = lax.dot_general(
            grad_qkv, w_qkv, (((1,), (1,)), ((), ())), preferred_element_type=f32
        )
        grad_gain_one = jnp.sum(grad_normed_one * normal_all, axis=0)
        own_grad_one = scatter_t(grad_normed_one.astype(bf16))
        sums = jnp.concatenate(
            [grad_router_part, grad_gain_one[:, None], grad_gain_two[:, None]], axis=1
        )
        (sums,) = tie(
            jnp.concatenate(
                [*split(sums), jnp.zeros((width, side_cols - 2 * n_experts - 4), bf16)], axis=1
            )
        )
        grad_attn = jnp.concatenate(
            [
                lax.dot_general(
                    normed_one, grad_qkv, contract_rows, preferred_element_type=f32
                ).astype(bf16),
                grad_out_part,
                sums,
            ],
            axis=1,
        )
        shard_attn = lax.psum_scatter(by_rows(grad_attn), dp, scatter_dimension=0, tiled=True)
        shard_attn = shard_attn.astype(f32)
        grad_input_part, _ = norm_backward(tokens_f, rms_scale(tokens_f), gain_one, own_grad_one)
        grad_tokens = grad_middle + grad_input_part
        side_sum = shard_attn[:, attn_cols : attn_cols + 2 * n_experts + 4]
        side_sum = sum_tensor(jnp.sum(side_sum.reshape(depth, 2, -1), axis=1).T)

        sent_gate_up[1], sent_gate_up[3], own_grad_one = tie(
            sent_gate_up[1], sent_gate_up[3], own_grad_one
        )
        grad_gate = jnp.zeros((n_experts, depth, hidden), f32)
        grad_up = grad_gate
        for shift in range(inner):
            start = (me_i - shift) % inner * own_experts
            gate, up = (
                jnp.swapaxes(part.reshape(depth, own_experts, hidden), 0, 1).astype(f32)
                for part in sent_gate_up[shift]
            )
            grad_gate = put(grad_gate, gate, start, 0, 0)
            grad_up = put(grad_up, up, start, 0, 0)
        return (
            mixed,
            grad_tokens,
            side_sum[n_experts],
            shard_attn[:, :q_cols],
            shard_attn[:, q_cols : q_cols + k_cols],
            shard_attn[:, q_cols + k_cols : qkv_cols],
            shard_attn[:, qkv_cols:attn_cols].T,
            side_sum[n_experts + 1],
            side_sum[:n_experts].T,
            grad_gate,
            grad_up,
            grad_down,
        )

    in_specs = (
        P(("i", "o", "t"), None),
        P(("i", "o", "t"), None),
        P(dp),
        P(dp, None),
        P(dp),
        P(dp, "t"),
        P(dp, "t"),
        P(dp, "t"),
        P("t", dp),
        P(dp),
        P(dp, None),
        P(None, dp, "t"),
        P(None, dp, "t"),
        P(None, "t", dp),
    )
    out_specs = (
        P(("i", "o", "t"), None),
        P(("i", "o", "t"), None),
        P(dp),
        P(dp, "t"),
        P(dp, "t"),
        P(dp, "t"),
        P("t", dp),
        P(dp),
        P(dp, None),
        P(None, dp, "t"),
        P(None, dp, "t"),
        P(None, "t", dp),
    )
    return jax.shard_map(
        on_device, mesh=grid, in_specs=in_specs, out_specs=out_specs, check_vma=False
    )
```

```python
import jax
import jax.numpy as jnp
from jax import lax
from jax.experimental.layout import Layout, with_layout_constraint
from jax.sharding import Mesh, PartitionSpec as P

HEAD_DIM = 64
EPSILON = 1e-05
LANES = 128
HIGHEST = lax.Precision.HIGHEST
f32 = jnp.float32
bf16 = jnp.bfloat16


def rms_scale(values):
    return lax.rsqrt(jnp.mean(values * values, axis=-1, keepdims=True) + EPSILON)


def norm_backward(values, scale, gain, grad_normed):
    normal_x = values * scale
    grad_hat = grad_normed * gain
    grad_values = scale * (
        grad_hat - normal_x * jnp.mean(grad_hat * normal_x, axis=-1, keepdims=True)
    )
    return grad_values, normal_x


def rotary_tables(row_count, half):
    position = jnp.arange(row_count, dtype=jnp.int32).astype(f32)
    inverse = jnp.power(10000.0, -jnp.arange(half, dtype=jnp.int32).astype(f32) / half)
    angle = position[:, None] * inverse[None, :]
    return jnp.cos(angle)[:, None, :], jnp.sin(angle)[:, None, :]


def rotate(tensor, cosine, sine):
    half = tensor.shape[-1] // 2
    first = tensor[..., :half]
    second = tensor[..., half:]
    return jnp.concatenate(
        [first * cosine - second * sine, second * cosine + first * sine], axis=-1
    )


def tie(*values):
    return lax.optimization_barrier(values)


def masked_scores(query, keys, prefix_len):
    seq_len, heads_kv, head_size = keys.shape
    grouped = query.reshape(seq_len, heads_kv, -1, head_size)
    scores = jnp.einsum(
        "qhgd,khd->hgqk", grouped, keys, preferred_element_type=f32
    ) * head_size ** (-0.5)
    row_ids = jnp.arange(seq_len, dtype=jnp.int32)
    allowed = (row_ids[None, :] <= row_ids[:, None]) | (row_ids[None, :] < prefix_len)
    return jnp.where(allowed, scores, -1e30), grouped


def attend_forward(query, keys, values, prefix_len):
    scores, _ = masked_scores(query, keys, prefix_len)
    highest = jnp.max(scores, axis=-1, keepdims=True)
    shifted = jnp.exp(scores - highest)
    summed = jnp.sum(shifted, axis=-1, keepdims=True)
    weights = (shifted / summed).astype(bf16)
    output = jnp.einsum("hgqk,khd->qhgd", weights, values, preferred_element_type=f32)
    return output.reshape(query.shape[0], -1).astype(bf16), highest + jnp.log(summed)


def attend_backward(query, keys, values, grad_mixed, log_total, prefix_len, hold):
    scores, grouped = masked_scores(query, keys, prefix_len)
    weights = jnp.exp(scores - log_total)
    seq_len, heads_kv, head_size = keys.shape
    grad_grouped = grad_mixed.reshape(seq_len, heads_kv, -1, head_size)
    grad_weights = jnp.einsum(
        "qhgd,khd->hgqk", grad_grouped, values, preferred_element_type=f32
    )
    grad_scores = (
        weights * (grad_weights - jnp.sum(weights * grad_weights, axis=-1, keepdims=True))
    ).astype(bf16)
    grad_scores, hold = tie(grad_scores, hold)
    scaling = head_size ** (-0.5)
    grad_query = (
        jnp.einsum("hgqk,khd->qhgd", grad_scores, keys, preferred_element_type=f32) * scaling
    )
    grad_keys = (
        jnp.einsum("hgqk,qhgd->khd", grad_scores, grouped, preferred_element_type=f32) * scaling
    )
    grad_values = jnp.einsum(
        "hgqk,qhgd->khd", weights.astype(bf16), grad_grouped, preferred_element_type=f32
    )
    return grad_query.reshape(seq_len, -1, head_size), grad_keys, grad_values, hold


def swap(values, axis, size, bit):
    return lax.ppermute(values, axis, [(m, m ^ bit) for m in range(size)])


def by_rows(values):
    return with_layout_constraint(values, Layout(major_to_minor=(0, 1)))


def split(values):
    high = values.astype(bf16)
    return high, (values - high.astype(f32)).astype(bf16)


def put(result, piece, *starts):
    return lax.dynamic_update_slice(result, piece, starts)


def solution(mesh):
    n_dp, n_tensor = mesh.shape["dp"], mesh.shape["tensor"]
    inner = 4
    outer = n_dp // inner
    grid = Mesh(mesh.devices.reshape(inner, outer, n_tensor), ("i", "o", "t"))
    dp = ("i", "o")
    shared = ("i", "t")

    def to_owner_order(values):
        rows = values.shape[0]
        if outer == 1:
            return values
        split = jnp.swapaxes(values.reshape(rows, inner, outer, -1), 1, 2)
        if outer == 2:
            split = jnp.where(lax.axis_index("o") == 0, split, split[:, ::-1])
        return split.reshape(rows, -1)

    def from_owner_order(values):
        rows = values.shape[0]
        if outer == 1:
            return values
        split = values.reshape(rows, outer, inner, -1)
        if outer == 2:
            split = jnp.where(lax.axis_index("o") == 0, split, split[:, ::-1])
        return jnp.swapaxes(split, 1, 2).reshape(rows, -1)

    def pass_on(pair):
        if outer == 2:
            return tuple(jnp.stack([piece, swap(piece, "o", 2, 1)]) for piece in pair)
        return tuple(lax.all_gather(piece, "o", axis=0) for piece in pair)

    def sum_outer(parts):
        if outer == 1:
            return parts[0]
        if outer == 2:
            return (parts[0].astype(f32) + swap(parts[1], "o", 2, 1).astype(f32)).astype(bf16)
        return lax.psum_scatter(parts, "o", scatter_dimension=0, tiled=False)

    def gather_t(block, hold=()):
        if n_tensor != 4:
            return tie(lax.all_gather(block, "t", axis=0, tiled=True), hold)
        rows, width = block.shape
        me_t = lax.axis_index("t")
        result = jnp.zeros((n_tensor * rows, width), block.dtype)
        pair = jnp.concatenate([block, swap(block, "t", n_tensor, 2)], axis=0)
        pair, hold = tie(pair, hold)
        for bit, part in ((0, pair), (1, swap(pair, "t", n_tensor, 1))):
            result = put(result, part[:rows], (me_t ^ bit) * rows, 0)
            result = put(result, part[rows:], (me_t ^ bit ^ 2) * rows, 0)
        return result, hold

    def scatter_t(values):
        if n_tensor != 4:
            return lax.psum_scatter(values, "t", scatter_dimension=0, tiled=True).astype(f32)
        me_t = lax.axis_index("t")
        block = values.reshape(2, 2, -1, values.shape[1])
        for axis, bit, own in ((1, 1, me_t % 2), (0, 2, me_t // 2)):
            keep = lax.dynamic_index_in_dim(block, own, axis, keepdims=False)
            send = lax.dynamic_index_in_dim(block, 1 - own, axis, keepdims=False)
            block = keep.astype(f32) + swap(send.astype(bf16), "t", n_tensor, bit).astype(f32)
        return block

    def sum_tensor(values):
        me_t = lax.axis_index("t")
        slots = put(jnp.zeros((n_tensor, *values.shape), f32), values[None], me_t, 0, 0)
        for shift in range(1, n_tensor):
            got = lax.ppermute(values, "t", [(m, (m + shift) % n_tensor) for m in range(n_tensor)])
            slots = put(slots, got[None], (me_t - shift) % n_tensor, 0, 0)
        return jnp.sum(slots, axis=0)

    def on_device(
        tokens,
        cotangent,
        prefix,
        routes,
        norm1,
        w_query,
        w_key,
        w_value,
        w_out,
        norm2,
        w_router,
        w_gate,
        w_up,
        w_down,
    ):
        rows, width = tokens.shape
        group = routes.shape[0]
        n_experts, depth, hidden = w_gate.shape
        own_experts = n_experts // inner
        own_hidden = own_experts * hidden
        q_cols, k_cols = w_query.shape[1], w_key.shape[1]
        qkv_cols = q_cols + 2 * k_cols
        attn_cols = qkv_cols + q_cols
        side_cols = -(-(2 * n_experts + 4) // LANES) * LANES
        gate_cols = -(-2 * n_experts // LANES) * LANES
        me_i, me_t = lax.axis_index("i"), lax.axis_index("t")

        side = jnp.concatenate(
            [
                w_router,
                norm1[:, None],
                norm2[:, None],
                jnp.zeros((depth, side_cols - n_experts - 2), bf16),
            ],
            axis=1,
        )
        pack = jnp.concatenate([w_query, w_key, w_value, w_out.T, side], axis=1)
        packed = lax.all_gather(pack, dp, axis=0, tiled=True)
        tokens_all, _ = gather_t(tokens)

        def expert_piece(target):
            first = target * own_experts
            gate, up = (
                jnp.swapaxes(lax.dynamic_slice_in_dim(w, first, own_experts, 0), 0, 1)
                for w in (w_gate, w_up)
            )
            down = lax.dynamic_slice_in_dim(w_down, first, own_experts, 0).transpose(2, 0, 1)
            gate_up = jnp.concatenate(
                [gate.reshape(depth, own_hidden), up.reshape(depth, own_hidden)], axis=1
            )
            return by_rows(gate_up), by_rows(down.reshape(depth, own_hidden))

        def to_owner(piece, shift):
            pairs = [(m, (m + shift) % inner) for m in range(inner)]
            return jax.tree.map(lambda part: lax.ppermute(part, "i", pairs), piece)

        pieces = [expert_piece((me_i + shift) % inner) for shift in range(inner)]
        pieces, packed = tie(pieces, packed)
        tokens_all = tokens_all.astype(f32)
        far_gate_up = to_owner(pieces[2][0], 2)
        owned = [pass_on(pieces[0])]

        w_qkv = packed[:, :qkv_cols]
        w_out_t = packed[:, qkv_cols:attn_cols]
        router = packed[:, attn_cols : attn_cols + n_experts]
        gains = packed[:, attn_cols + n_experts : attn_cols + n_experts + 2].astype(f32).T
        gain_one, gain_two = gains[0], gains[1]

        normal_all = tokens_all * rms_scale(tokens_all)
        normed_one = (normal_all * gain_one).astype(bf16)
        cosine, sine = rotary_tables(group, HEAD_DIM // 2)
        qkv = jnp.dot(normed_one, w_qkv, preferred_element_type=f32)
        query = rotate(qkv[:, :q_cols].reshape(group, -1, HEAD_DIM), cosine, sine).astype(bf16)
        keys = rotate(
            qkv[:, q_cols : q_cols + k_cols].reshape(group, -1, HEAD_DIM), cosine, sine
        ).astype(bf16)
        values = qkv[:, q_cols + k_cols :].astype(bf16).reshape(group, -1, HEAD_DIM)
        attended, log_total = attend_forward(query, keys, values, prefix[0])
        far_down, near, far_gate_up, owned[0], attended = tie(
            pieces[2][1], pieces[1], far_gate_up, owned[0], attended
        )
        far_down, near = to_owner(far_down, 2), to_owner(near, 1)
        branch = lax.dot_general(
            attended, w_out_t, (((1,), (1,)), ((), ())), preferred_element_type=f32
        ).astype(bf16)
        tokens_f = tokens.astype(f32)
        branch = scatter_t(branch)
        middle = tokens_f + branch
        scale_two = rms_scale(middle)
        normed_two = (middle * scale_two * gain_two).astype(bf16)

        logits = jnp.dot(normed_two, router, preferred_element_type=f32)
        own_routes = lax.dynamic_slice_in_dim(routes, me_t * rows, rows, 0)
        expert_ids = jnp.arange(n_experts, dtype=jnp.int32)
        routed = jnp.any(own_routes[:, :, None] == expert_ids[None, None, :], axis=1)
        gates = jnp.where(routed, jax.nn.softmax(jnp.where(routed, logits, -1e30), axis=-1), 0.0)
        gates_high = gates.astype(bf16)
        gates_low = (gates - gates_high.astype(f32)).astype(bf16)
        shipped = jnp.concatenate(
            [
                to_owner_order(normed_two),
                gates_high,
                gates_low,
                jnp.zeros((rows, gate_cols - 2 * n_experts), bf16),
            ],
            axis=1,
        )
        last, near, far_down, shipped = tie(pieces[3], near, far_down, shipped)
        last = to_owner(last, 3)
        owned += [pass_on(near), pass_on((far_gate_up, far_down)), pass_on(last)]
        shared_all = by_rows(lax.all_gather(by_rows(shipped), shared, axis=0, tiled=True))
        w_gate_up = jnp.zeros((outer, inner, depth, 2 * own_hidden), bf16)
        w_down_t = jnp.zeros((outer, inner, depth, own_hidden), bf16)
        for shift in range(inner):
            source = (me_i - shift) % inner
            w_gate_up = put(w_gate_up, owned[shift][0][:, None], 0, source, 0, 0)
            w_down_t = put(w_down_t, owned[shift][1][:, None], 0, source, 0, 0)
        cot_order, shared_all, w_gate_up, w_down_t = tie(
            by_rows(to_owner_order(cotangent)),
            shared_all,
            w_gate_up.reshape(outer * inner * depth, 2 * own_hidden),
            w_down_t.reshape(outer * inner * depth, own_hidden),
        )
        cot_all = by_rows(lax.all_gather(cot_order, shared, axis=0, tiled=True))
        count = shared_all.shape[0]
        normed_all = shared_all[:, :width]

        slot = jnp.arange(gate_cols, dtype=jnp.int32)[:, None]
        owner = me_i * own_experts + jnp.arange(own_hidden, dtype=jnp.int32)[None, :] // hidden
        spread = ((slot == owner) | (slot == owner + n_experts)).astype(bf16)
        gate_wide = jnp.dot(shared_all[:, width:], spread, preferred_element_type=f32)
        gate_up = jnp.dot(normed_all, w_gate_up, preferred_element_type=f32).astype(bf16)
        gate_up, gate_wide = tie(gate_up, gate_wide.astype(bf16))

        def activate(gate_up):
            gate_part = gate_up[:, :own_hidden].astype(f32)
            up_part = gate_up[:, own_hidden:].astype(f32)
            sigmoid_g = jax.nn.sigmoid(gate_part)
            return gate_part, up_part, sigmoid_g, gate_part * sigmoid_g

        _, up_part, _, silu_g = activate(gate_up)
        gated = (silu_g * up_part * gate_wide.astype(f32)).astype(bf16)
        expert_part = lax.dot_general(
            gated, w_down_t, (((1,), (1,)), ((), ())), preferred_element_type=f32
        ).astype(bf16)
        expert_part, cot_all, gate_up, gate_wide = tie(
            by_rows(expert_part), cot_all, gate_up, gate_wide
        )
        expert_share = lax.psum_scatter(expert_part, shared, scatter_dimension=0, tiled=True)
        contract_rows = (((0,), (0,)), ((), ()))
        grad_w_down = lax.dot_general(
            cot_all, gated, contract_rows, preferred_element_type=f32
        ).astype(bf16)
        grad_w_down, cot_all = tie(grad_w_down, cot_all)

        def to_sum(grad):
            by_owner = grad.reshape(outer, inner, depth, -1)
            return [
                sum_outer(
                    lax.dynamic_index_in_dim(by_owner, (me_i + shift) % inner, 1, keepdims=False)
                )
                for shift in range(inner)
            ]

        down_sums = to_sum(grad_w_down)
        cot_part = jnp.dot(cot_all, w_down_t, preferred_element_type=f32)
        gate_part, up_part, sigmoid_g, silu_g = activate(gate_up)
        grad_act = cot_part * gate_wide.astype(f32)
        grad_gate_up = jnp.concatenate(
            [
                (grad_act * up_part * sigmoid_g * (1.0 + gate_part * (1.0 - sigmoid_g))).astype(
                    bf16
                ),
                (grad_act * silu_g).astype(bf16),
            ],
            axis=1,
        )
        products, down_sums, w_gate_up = tie(
            (silu_g * up_part * cot_part).astype(bf16), down_sums, w_gate_up
        )
        sent_down = down_sums[:1] + [to_owner(down_sums[s], s) for s in range(1, inner)]
        chosen = (jnp.arange(side_cols, dtype=jnp.int32)[None, :] == owner.T).astype(bf16)
        gate_block = jnp.dot(products, chosen, preferred_element_type=f32)
        grad_normed_part = lax.dot_general(
            grad_gate_up, w_gate_up, (((1,), (1,)), ((), ())), preferred_element_type=f32
        )
        grad_shipped = jnp.concatenate([grad_normed_part, gate_block], axis=1).astype(bf16)
        grad_shipped, sent_down, expert_share = tie(by_rows(grad_shipped), sent_down, expert_share)
        grad_back = lax.psum_scatter(grad_shipped, shared, scatter_dimension=0, tiled=True)
        shared_rows, _ = tie(shared_all, grad_shipped)
        grad_w_gate_up = lax.dot_general(
            shared_rows[:, :width], grad_gate_up, contract_rows, preferred_element_type=f32
        ).astype(bf16)
        gate_up_sums = to_sum(grad_w_gate_up)
        grad_down = jnp.zeros((n_experts, hidden, depth), f32)
        for shift in range(inner):
            part = sent_down[shift].reshape(depth, own_experts, hidden).transpose(1, 2, 0)
            grad_down = put(
                grad_down, part.astype(f32), (me_i - shift) % inner * own_experts, 0, 0
            )
        gate_up_sums, grad_down, grad_back = tie(gate_up_sums, grad_down, grad_back)
        far_sum_gate, far_sum_up = jnp.split(gate_up_sums[2], 2, axis=1)
        sent_gate_up = {0: jnp.split(gate_up_sums[0], 2, axis=1)}
        mixed = (middle + from_owner_order(expert_share).astype(f32)).astype(bf16)

        grad_back = grad_back.astype(f32)
        grad_chosen = grad_back[:, width : width + n_experts]
        grad_logits = gates * (
            grad_chosen - jnp.sum(gates * grad_chosen, axis=-1, keepdims=True)
        )
        grad_normed_two = from_owner_order(grad_back[:, :width]) + jnp.dot(
            grad_logits, router.astype(f32).T, precision=HIGHEST
        )
        grad_middle_part, normal_two = norm_backward(
            middle, scale_two, gain_two, grad_normed_two
        )
        grad_middle = cotangent.astype(f32) + grad_middle_part
        grad_gain_two = jnp.sum(grad_normed_two * normal_two, axis=0)
        grad_router_part = lax.dot_general(
            normed_two.astype(f32), grad_logits, contract_rows, precision=HIGHEST
        )
        sent_gate = to_owner(far_sum_gate, 2)
        grad_branch, (sent_gate, far_sum_up) = gather_t(
            grad_middle.astype(bf16), (sent_gate, far_sum_up)
        )
        sent_up = to_owner(far_sum_up, 2)
        grad_out_part = lax.dot_general(
            grad_branch, attended, contract_rows, preferred_element_type=f32
        ).astype(bf16)
        grad_out_part, grad_branch = tie(grad_out_part, grad_branch)
        grad_attended = jnp.dot(
            grad_branch, w_out_t, preferred_element_type=f32
        ).astype(bf16)
        grad_query, grad_keys, grad_values, (sent_up, near_sum, last_sum) = attend_backward(
            query,
            keys,
            values,
            grad_attended,
            log_total,
            prefix[0],
            (sent_up, gate_up_sums[1], gate_up_sums[3]),
        )
        sent_gate_up[2] = (sent_gate, sent_up)
        sent_gate_up[1], sent_gate_up[3] = to_owner(near_sum, 1), to_owner(last_sum, 3)
        grad_query, grad_keys, grad_values, sent_gate_up[1] = tie(
            grad_query, grad_keys, grad_values, sent_gate_up[1]
        )
        for shift in (1, 3):
            sent_gate_up[shift] = jnp.split(sent_gate_up[shift], 2, axis=1)
        grad_qkv = jnp.concatenate(
            [
                rotate(grad_query, cosine, -sine).astype(bf16).reshape(group, -1),
                rotate(grad_keys, cosine, -sine).astype(bf16).reshape(group, -1),
                grad_values.astype(bf16).reshape(group, -1),
            ],
            axis=1,
        )
        grad_normed_one = lax.dot_general(
            grad_qkv, w_qkv, (((1,), (1,)), ((), ())), preferred_element_type=f32
        )
        grad_gain_one = jnp.sum(grad_normed_one * normal_all, axis=0)
        own_grad_one = scatter_t(grad_normed_one.astype(bf16))
        sums = jnp.concatenate(
            [grad_router_part, grad_gain_one[:, None], grad_gain_two[:, None]], axis=1
        )
        (sums,) = tie(
            jnp.concatenate(
                [*split(sums), jnp.zeros((width, side_cols - 2 * n_experts - 4), bf16)], axis=1
            )
        )
        grad_attn = jnp.concatenate(
            [
                lax.dot_general(
                    normed_one, grad_qkv, contract_rows, preferred_element_type=f32
                ).astype(bf16),
                grad_out_part,
                sums,
            ],
            axis=1,
        )
        shard_attn = lax.psum_scatter(by_rows(grad_attn), dp, scatter_dimension=0, tiled=True)
        shard_attn = shard_attn.astype(f32)
        grad_input_part, _ = norm_backward(tokens_f, rms_scale(tokens_f), gain_one, own_grad_one)
        grad_tokens = grad_middle + grad_input_part
        side_sum = shard_attn[:, attn_cols : attn_cols + 2 * n_experts + 4]
        side_sum = sum_tensor(jnp.sum(side_sum.reshape(depth, 2, -1), axis=1).T)

        sent_gate_up[1], sent_gate_up[3], own_grad_one = tie(
            sent_gate_up[1], sent_gate_up[3], own_grad_one
        )
        grad_gate = jnp.zeros((n_experts, depth, hidden), f32)
        grad_up = grad_gate
        for shift in range(inner):
            start = (me_i - shift) % inner * own_experts
            gate, up = (
                jnp.swapaxes(part.reshape(depth, own_experts, hidden), 0, 1).astype(f32)
                for part in sent_gate_up[shift]
            )
            grad_gate = put(grad_gate, gate, start, 0, 0)
            grad_up = put(grad_up, up, start, 0, 0)
        return (
            mixed,
            grad_tokens,
            side_sum[n_experts],
            shard_attn[:, :q_cols],
            shard_attn[:, q_cols : q_cols + k_cols],
            shard_attn[:, q_cols + k_cols : qkv_cols],
            shard_attn[:, qkv_cols:attn_cols].T,
            side_sum[n_experts + 1],
            side_sum[:n_experts].T,
            grad_gate,
            grad_up,
            grad_down,
        )

    in_specs = (
        P(("i", "o", "t"), None),
        P(("i", "o", "t"), None),
        P(dp),
        P(dp, None),
        P(dp),
        P(dp, "t"),
        P(dp, "t"),
        P(dp, "t"),
        P("t", dp),
        P(dp),
        P(dp, None),
        P(None, dp, "t"),
        P(None, dp, "t"),
        P(None, "t", dp),
    )
    out_specs = (
        P(("i", "o", "t"), None),
        P(("i", "o", "t"), None),
        P(dp),
        P(dp, "t"),
        P(dp, "t"),
        P(dp, "t"),
        P("t", dp),
        P(dp),
        P(dp, None),
        P(None, dp, "t"),
        P(None, dp, "t"),
        P(None, "t", dp),
    )
    return jax.shard_map(
        on_device, mesh=grid, in_specs=in_specs, out_specs=out_specs, check_vma=False
    )
```

```python
import jax
import jax.numpy as jnp
from jax import lax
from jax.experimental.layout import Layout, with_layout_constraint
from jax.sharding import Mesh, PartitionSpec as P

HEAD_DIM = 64
EPSILON = 1e-05
LANES = 128
HIGHEST = lax.Precision.HIGHEST
f32 = jnp.float32
bf16 = jnp.bfloat16


def rms_scale(values):
    return lax.rsqrt(jnp.mean(values * values, axis=-1, keepdims=True) + EPSILON)


def norm_backward(values, scale, gain, grad_normed):
    normal_x = values * scale
    grad_hat = grad_normed * gain
    grad_values = scale * (
        grad_hat - normal_x * jnp.mean(grad_hat * normal_x, axis=-1, keepdims=True)
    )
    return grad_values, normal_x


def rotary_tables(row_count, half):
    position = jnp.arange(row_count, dtype=jnp.int32).astype(f32)
    inverse = jnp.power(10000.0, -jnp.arange(half, dtype=jnp.int32).astype(f32) / half)
    angle = position[:, None] * inverse[None, :]
    return jnp.cos(angle)[:, None, :], jnp.sin(angle)[:, None, :]


def rotate(tensor, cosine, sine):
    half = tensor.shape[-1] // 2
    first = tensor[..., :half]
    second = tensor[..., half:]
    return jnp.concatenate(
        [first * cosine - second * sine, second * cosine + first * sine], axis=-1
    )


def tie(*values):
    return lax.optimization_barrier(values)


def masked_scores(query, keys, prefix_len):
    seq_len, heads_kv, head_size = keys.shape
    grouped = query.reshape(seq_len, heads_kv, -1, head_size)
    scores = jnp.einsum(
        "qhgd,khd->hgqk", grouped, keys, preferred_element_type=f32
    ) * head_size ** (-0.5)
    row_ids = jnp.arange(seq_len, dtype=jnp.int32)
    allowed = (row_ids[None, :] <= row_ids[:, None]) | (row_ids[None, :] < prefix_len)
    return jnp.where(allowed, scores, -1e30), grouped


def attend_forward(query, keys, values, prefix_len):
    scores, _ = masked_scores(query, keys, prefix_len)
    highest = jnp.max(scores, axis=-1, keepdims=True)
    shifted = jnp.exp(scores - highest)
    summed = jnp.sum(shifted, axis=-1, keepdims=True)
    weights = (shifted / summed).astype(bf16)
    output = jnp.einsum("hgqk,khd->qhgd", weights, values, preferred_element_type=f32)
    return output.reshape(query.shape[0], -1).astype(bf16), highest + jnp.log(summed)


def attend_backward(query, keys, values, grad_mixed, log_total, prefix_len, hold):
    scores, grouped = masked_scores(query, keys, prefix_len)
    weights = jnp.exp(scores - log_total)
    seq_len, heads_kv, head_size = keys.shape
    grad_grouped = grad_mixed.reshape(seq_len, heads_kv, -1, head_size)
    grad_weights = jnp.einsum(
        "qhgd,khd->hgqk", grad_grouped, values, preferred_element_type=f32
    )
    grad_scores = (
        weights * (grad_weights - jnp.sum(weights * grad_weights, axis=-1, keepdims=True))
    ).astype(bf16)
    grad_scores, hold = tie(grad_scores, hold)
    scaling = head_size ** (-0.5)
    grad_query = (
        jnp.einsum("hgqk,khd->qhgd", grad_scores, keys, preferred_element_type=f32) * scaling
    )
    grad_keys = (
        jnp.einsum("hgqk,qhgd->khd", grad_scores, grouped, preferred_element_type=f32) * scaling
    )
    grad_values = jnp.einsum(
        "hgqk,qhgd->khd", weights.astype(bf16), grad_grouped, preferred_element_type=f32
    )
    return grad_query.reshape(seq_len, -1, head_size), grad_keys, grad_values, hold


def swap(values, axis, size, bit):
    return lax.ppermute(values, axis, [(m, m ^ bit) for m in range(size)])


def by_rows(values):
    return with_layout_constraint(values, Layout(major_to_minor=(0, 1)))


def split(values):
    high = values.astype(bf16)
    return high, (values - high.astype(f32)).astype(bf16)


def put(result, piece, *starts):
    return lax.dynamic_update_slice(result, piece, starts)


def solution(mesh):
    n_dp, n_tensor = mesh.shape["dp"], mesh.shape["tensor"]
    inner = 4
    outer = n_dp // inner
    grid = Mesh(mesh.devices.reshape(inner, outer, n_tensor), ("i", "o", "t"))
    dp = ("i", "o")
    shared = ("i", "t")

    def to_owner_order(values):
        rows = values.shape[0]
        if outer == 1:
            return values
        split = jnp.swapaxes(values.reshape(rows, inner, outer, -1), 1, 2)
        if outer == 2:
            split = jnp.where(lax.axis_index("o") == 0, split, split[:, ::-1])
        return split.reshape(rows, -1)

    def from_owner_order(values):
        rows = values.shape[0]
        if outer == 1:
            return values
        split = values.reshape(rows, outer, inner, -1)
        if outer == 2:
            split = jnp.where(lax.axis_index("o") == 0, split, split[:, ::-1])
        return jnp.swapaxes(split, 1, 2).reshape(rows, -1)

    def pass_on(pair):
        if outer == 2:
            return tuple(jnp.stack([piece, swap(piece, "o", 2, 1)]) for piece in pair)
        return tuple(lax.all_gather(piece, "o", axis=0) for piece in pair)

    def sum_outer(parts):
        if outer == 1:
            return parts[0]
        if outer == 2:
            return (parts[0].astype(f32) + swap(parts[1], "o", 2, 1).astype(f32)).astype(bf16)
        return lax.psum_scatter(parts, "o", scatter_dimension=0, tiled=False)

    def gather_t(block, hold=()):
        if n_tensor != 4:
            return tie(lax.all_gather(block, "t", axis=0, tiled=True), hold)
        rows, width = block.shape
        me_t = lax.axis_index("t")
        result = jnp.zeros((n_tensor * rows, width), block.dtype)
        pair = jnp.concatenate([block, swap(block, "t", n_tensor, 2)], axis=0)
        pair, hold = tie(pair, hold)
        for bit, part in ((0, pair), (1, swap(pair, "t", n_tensor, 1))):
            result = put(result, part[:rows], (me_t ^ bit) * rows, 0)
            result = put(result, part[rows:], (me_t ^ bit ^ 2) * rows, 0)
        return result, hold

    def scatter_t(values):
        if n_tensor != 4:
            return lax.psum_scatter(values, "t", scatter_dimension=0, tiled=True).astype(f32)
        me_t = lax.axis_index("t")
        block = values.reshape(2, 2, -1, values.shape[1])
        for axis, bit, own in ((1, 1, me_t % 2), (0, 2, me_t // 2)):
            keep = lax.dynamic_index_in_dim(block, own, axis, keepdims=False)
            send = lax.dynamic_index_in_dim(block, 1 - own, axis, keepdims=False)
            block = keep.astype(f32) + swap(send.astype(bf16), "t", n_tensor, bit).astype(f32)
        return block

    def scatter_small(values):
        if n_tensor != 4:
            return lax.psum_scatter(values, shared, scatter_dimension=0, tiled=True).astype(f32)
        me_i, me_t = lax.axis_index("i"), lax.axis_index("t")
        block = values.reshape(inner, 2, 2, -1, values.shape[1])
        for axis, bit, own in ((2, 1, me_t % 2), (1, 2, me_t // 2)):
            keep = lax.dynamic_index_in_dim(block, own, axis, keepdims=False)
            send = lax.dynamic_index_in_dim(block, 1 - own, axis, keepdims=False)
            block = (keep.astype(f32) + swap(send, "t", n_tensor, bit).astype(f32)).astype(bf16)
        total = lax.dynamic_index_in_dim(block, me_i, 0, keepdims=False).astype(f32)
        for shift in range(1, inner):
            send = lax.dynamic_index_in_dim(block, (me_i + shift) % inner, 0, keepdims=False)
            pairs = [(m, (m + shift) % inner) for m in range(inner)]
            total = total + lax.ppermute(send, "i", pairs).astype(f32)
        return total

    def sum_tensor(values):
        me_t = lax.axis_index("t")
        slots = put(jnp.zeros((n_tensor, *values.shape), f32), values[None], me_t, 0, 0)
        for shift in range(1, n_tensor):
            got = lax.ppermute(values, "t", [(m, (m + shift) % n_tensor) for m in range(n_tensor)])
            slots = put(slots, got[None], (me_t - shift) % n_tensor, 0, 0)
        return jnp.sum(slots, axis=0)

    def on_device(
        tokens,
        cotangent,
        prefix,
        routes,
        norm1,
        w_query,
        w_key,
        w_value,
        w_out,
        norm2,
        w_router,
        w_gate,
        w_up,
        w_down,
    ):
        rows, width = tokens.shape
        group = routes.shape[0]
        n_experts, depth, hidden = w_gate.shape
        own_experts = n_experts // inner
        own_hidden = own_experts * hidden
        q_cols, k_cols = w_query.shape[1], w_key.shape[1]
        qkv_cols = q_cols + 2 * k_cols
        attn_cols = qkv_cols + q_cols
        side_cols = -(-(2 * n_experts + 4) // LANES) * LANES
        gate_cols = -(-2 * n_experts // LANES) * LANES
        me_i, me_t = lax.axis_index("i"), lax.axis_index("t")

        side = jnp.concatenate(
            [
                w_router,
                norm1[:, None],
                norm2[:, None],
                jnp.zeros((depth, side_cols - n_experts - 2), bf16),
            ],
            axis=1,
        )
        pack = jnp.concatenate([w_query, w_key, w_value, w_out.T, side], axis=1)
        packed = lax.all_gather(pack, dp, axis=0, tiled=True)
        tokens_all, _ = gather_t(tokens)

        def expert_piece(target):
            first = target * own_experts
            gate, up = (
                jnp.swapaxes(lax.dynamic_slice_in_dim(w, first, own_experts, 0), 0, 1)
                for w in (w_gate, w_up)
            )
            down = lax.dynamic_slice_in_dim(w_down, first, own_experts, 0).transpose(2, 0, 1)
            gate_up = jnp.concatenate(
                [gate.reshape(depth, own_hidden), up.reshape(depth, own_hidden)], axis=1
            )
            return by_rows(gate_up), by_rows(down.reshape(depth, own_hidden))

        def to_owner(piece, shift):
            pairs = [(m, (m + shift) % inner) for m in range(inner)]
            return jax.tree.map(lambda part: lax.ppermute(part, "i", pairs), piece)

        pieces = [expert_piece((me_i + shift) % inner) for shift in range(inner)]
        pieces, packed = tie(pieces, packed)
        tokens_all = tokens_all.astype(f32)
        far_gate_up = to_owner(pieces[2][0], 2)
        owned = [pass_on(pieces[0])]

        w_qkv = packed[:, :qkv_cols]
        w_out_t = packed[:, qkv_cols:attn_cols]
        router = packed[:, attn_cols : attn_cols + n_experts]
        gains = packed[:, attn_cols + n_experts : attn_cols + n_experts + 2].astype(f32).T
        gain_one, gain_two = gains[0], gains[1]

        normal_all = tokens_all * rms_scale(tokens_all)
        normed_one = (normal_all * gain_one).astype(bf16)
        cosine, sine = rotary_tables(group, HEAD_DIM // 2)
        qkv = jnp.dot(normed_one, w_qkv, preferred_element_type=f32)
        query = rotate(qkv[:, :q_cols].reshape(group, -1, HEAD_DIM), cosine, sine).astype(bf16)
        keys = rotate(
            qkv[:, q_cols : q_cols + k_cols].reshape(group, -1, HEAD_DIM), cosine, sine
        ).astype(bf16)
        values = qkv[:, q_cols + k_cols :].astype(bf16).reshape(group, -1, HEAD_DIM)
        attended, log_total = attend_forward(query, keys, values, prefix[0])
        far_down, near, far_gate_up, owned[0], attended = tie(
            pieces[2][1], pieces[1], far_gate_up, owned[0], attended
        )
        far_down, near = to_owner(far_down, 2), to_owner(near, 1)
        branch = lax.dot_general(
            attended, w_out_t, (((1,), (1,)), ((), ())), preferred_element_type=f32
        ).astype(bf16)
        tokens_f = tokens.astype(f32)
        branch = scatter_t(branch)
        middle = tokens_f + branch
        scale_two = rms_scale(middle)
        normed_two = (middle * scale_two * gain_two).astype(bf16)

        logits = jnp.dot(normed_two, router, preferred_element_type=f32)
        own_routes = lax.dynamic_slice_in_dim(routes, me_t * rows, rows, 0)
        expert_ids = jnp.arange(n_experts, dtype=jnp.int32)
        routed = jnp.any(own_routes[:, :, None] == expert_ids[None, None, :], axis=1)
        gates = jnp.where(routed, jax.nn.softmax(jnp.where(routed, logits, -1e30), axis=-1), 0.0)
        gates_high = gates.astype(bf16)
        gates_low = (gates - gates_high.astype(f32)).astype(bf16)
        shipped = jnp.concatenate(
            [
                to_owner_order(normed_two),
                gates_high,
                gates_low,
                jnp.zeros((rows, gate_cols - 2 * n_experts), bf16),
            ],
            axis=1,
        )
        last, near, far_down, shipped = tie(pieces[3], near, far_down, shipped)
        last = to_owner(last, 3)
        owned += [pass_on(near), pass_on((far_gate_up, far_down)), pass_on(last)]
        shared_all = by_rows(lax.all_gather(by_rows(shipped), shared, axis=0, tiled=True))
        w_gate_up = jnp.zeros((outer, inner, depth, 2 * own_hidden), bf16)
        w_down_t = jnp.zeros((outer, inner, depth, own_hidden), bf16)
        for shift in range(inner):
            source = (me_i - shift) % inner
            w_gate_up = put(w_gate_up, owned[shift][0][:, None], 0, source, 0, 0)
            w_down_t = put(w_down_t, owned[shift][1][:, None], 0, source, 0, 0)
        cot_order, shared_all, w_gate_up, w_down_t = tie(
            by_rows(to_owner_order(cotangent)),
            shared_all,
            w_gate_up.reshape(outer * inner * depth, 2 * own_hidden),
            w_down_t.reshape(outer * inner * depth, own_hidden),
        )
        cot_all = by_rows(lax.all_gather(cot_order, shared, axis=0, tiled=True))
        count = shared_all.shape[0]
        normed_all = shared_all[:, :width]

        slot = jnp.arange(gate_cols, dtype=jnp.int32)[:, None]
        owner = me_i * own_experts + jnp.arange(own_hidden, dtype=jnp.int32)[None, :] // hidden
        spread = ((slot == owner) | (slot == owner + n_experts)).astype(bf16)
        gate_wide = jnp.dot(shared_all[:, width:], spread, preferred_element_type=f32)
        gate_up = jnp.dot(normed_all, w_gate_up, preferred_element_type=f32).astype(bf16)
        gate_up, gate_wide = tie(gate_up, gate_wide.astype(bf16))

        def activate(gate_up):
            gate_part = gate_up[:, :own_hidden].astype(f32)
            up_part = gate_up[:, own_hidden:].astype(f32)
            sigmoid_g = jax.nn.sigmoid(gate_part)
            return gate_part, up_part, sigmoid_g, gate_part * sigmoid_g

        _, up_part, _, silu_g = activate(gate_up)
        gated = (silu_g * up_part * gate_wide.astype(f32)).astype(bf16)
        expert_part = lax.dot_general(
            gated, w_down_t, (((1,), (1,)), ((), ())), preferred_element_type=f32
        ).astype(bf16)
        expert_part, cot_all, gate_up, gate_wide = tie(
            by_rows(expert_part), cot_all, gate_up, gate_wide
        )
        expert_share = lax.psum_scatter(expert_part, shared, scatter_dimension=0, tiled=True)
        contract_rows = (((0,), (0,)), ((), ()))
        grad_w_down = lax.dot_general(
            cot_all, gated, contract_rows, preferred_element_type=f32
        ).astype(bf16)
        grad_w_down, cot_all = tie(grad_w_down, cot_all)

        def to_sum(grad):
            by_owner = grad.reshape(outer, inner, depth, -1)
            return [
                sum_outer(
                    lax.dynamic_index_in_dim(by_owner, (me_i + shift) % inner, 1, keepdims=False)
                )
                for shift in range(inner)
            ]

        down_sums = to_sum(grad_w_down)
        cot_part = jnp.dot(cot_all, w_down_t, preferred_element_type=f32)
        gate_part, up_part, sigmoid_g, silu_g = activate(gate_up)
        grad_act = cot_part * gate_wide.astype(f32)
        grad_gate_up = jnp.concatenate(
            [
                (grad_act * up_part * sigmoid_g * (1.0 + gate_part * (1.0 - sigmoid_g))).astype(
                    bf16
                ),
                (grad_act * silu_g).astype(bf16),
            ],
            axis=1,
        )
        products, down_sums, w_gate_up = tie(
            (silu_g * up_part * cot_part).astype(bf16), down_sums, w_gate_up
        )
        sent_down = down_sums[:1] + [to_owner(down_sums[s], s) for s in range(1, inner)]
        chosen = (jnp.arange(side_cols, dtype=jnp.int32)[None, :] == owner.T).astype(bf16)
        gate_block = jnp.dot(products, chosen, preferred_element_type=f32)
        grad_normed_part = lax.dot_general(
            grad_gate_up, w_gate_up, (((1,), (1,)), ((), ())), preferred_element_type=f32
        )
        gate_block, grad_shipped, sent_down, expert_share = tie(
            gate_block.astype(bf16),
            by_rows(grad_normed_part.astype(bf16)),
            sent_down,
            expert_share,
        )
        grad_back = lax.psum_scatter(grad_shipped, shared, scatter_dimension=0, tiled=True)
        shared_rows, _ = tie(shared_all, grad_shipped)
        grad_w_gate_up = lax.dot_general(
            shared_rows[:, :width], grad_gate_up, contract_rows, preferred_element_type=f32
        ).astype(bf16)
        gate_up_sums = to_sum(grad_w_gate_up)
        grad_down = jnp.zeros((n_experts, hidden, depth), f32)
        for shift in range(inner):
            part = sent_down[shift].reshape(depth, own_experts, hidden).transpose(1, 2, 0)
            grad_down = put(
                grad_down, part.astype(f32), (me_i - shift) % inner * own_experts, 0, 0
            )
        gates_back = scatter_small(gate_block)
        gate_up_sums, grad_down, gates_back, grad_back = tie(
            gate_up_sums, grad_down, gates_back, grad_back
        )
        far_sum_gate, far_sum_up = jnp.split(gate_up_sums[2], 2, axis=1)
        sent_gate_up = {0: jnp.split(gate_up_sums[0], 2, axis=1)}
        mixed = (middle + from_owner_order(expert_share).astype(f32)).astype(bf16)

        grad_back = grad_back.astype(f32)
        grad_chosen = gates_back[:, :n_experts]
        grad_logits = gates * (
            grad_chosen - jnp.sum(gates * grad_chosen, axis=-1, keepdims=True)
        )
        grad_normed_two = from_owner_order(grad_back) + jnp.dot(
            grad_logits, router.astype(f32).T, precision=HIGHEST
        )
        grad_middle_part, normal_two = norm_backward(
            middle, scale_two, gain_two, grad_normed_two
        )
        grad_middle = cotangent.astype(f32) + grad_middle_part
        grad_gain_two = jnp.sum(grad_normed_two * normal_two, axis=0)
        grad_router_part = lax.dot_general(
            normed_two.astype(f32), grad_logits, contract_rows, precision=HIGHEST
        )
        sent_gate = to_owner(far_sum_gate, 2)
        grad_branch, (sent_gate, far_sum_up) = gather_t(
            grad_middle.astype(bf16), (sent_gate, far_sum_up)
        )
        sent_up = to_owner(far_sum_up, 2)
        grad_out_part = lax.dot_general(
            grad_branch, attended, contract_rows, preferred_element_type=f32
        ).astype(bf16)
        grad_out_part, grad_branch = tie(grad_out_part, grad_branch)
        grad_attended = jnp.dot(
            grad_branch, w_out_t, preferred_element_type=f32
        ).astype(bf16)
        grad_query, grad_keys, grad_values, (sent_up, near_sum, last_sum) = attend_backward(
            query,
            keys,
            values,
            grad_attended,
            log_total,
            prefix[0],
            (sent_up, gate_up_sums[1], gate_up_sums[3]),
        )
        sent_gate_up[2] = (sent_gate, sent_up)
        sent_gate_up[1], sent_gate_up[3] = to_owner(near_sum, 1), to_owner(last_sum, 3)
        grad_query, grad_keys, grad_values, sent_gate_up[1] = tie(
            grad_query, grad_keys, grad_values, sent_gate_up[1]
        )
        for shift in (1, 3):
            sent_gate_up[shift] = jnp.split(sent_gate_up[shift], 2, axis=1)
        grad_qkv = jnp.concatenate(
            [
                rotate(grad_query, cosine, -sine).astype(bf16).reshape(group, -1),
                rotate(grad_keys, cosine, -sine).astype(bf16).reshape(group, -1),
                grad_values.astype(bf16).reshape(group, -1),
            ],
            axis=1,
        )
        grad_normed_one = lax.dot_general(
            grad_qkv, w_qkv, (((1,), (1,)), ((), ())), preferred_element_type=f32
        )
        grad_gain_one = jnp.sum(grad_normed_one * normal_all, axis=0)
        own_grad_one = scatter_t(grad_normed_one.astype(bf16))
        sums = jnp.concatenate(
            [grad_router_part, grad_gain_one[:, None], grad_gain_two[:, None]], axis=1
        )
        (sums,) = tie(
            jnp.concatenate(
                [*split(sums), jnp.zeros((width, side_cols - 2 * n_experts - 4), bf16)], axis=1
            )
        )
        grad_attn = jnp.concatenate(
            [
                lax.dot_general(
                    normed_one, grad_qkv, contract_rows, preferred_element_type=f32
                ).astype(bf16),
                grad_out_part,
                sums,
            ],
            axis=1,
        )
        shard_attn = lax.psum_scatter(by_rows(grad_attn), dp, scatter_dimension=0, tiled=True)
        shard_attn = shard_attn.astype(f32)
        grad_input_part, _ = norm_backward(tokens_f, rms_scale(tokens_f), gain_one, own_grad_one)
        grad_tokens = grad_middle + grad_input_part
        side_sum = shard_attn[:, attn_cols : attn_cols + 2 * n_experts + 4]
        side_sum = sum_tensor(jnp.sum(side_sum.reshape(depth, 2, -1), axis=1).T)

        sent_gate_up[1], sent_gate_up[3], own_grad_one = tie(
            sent_gate_up[1], sent_gate_up[3], own_grad_one
        )
        grad_gate = jnp.zeros((n_experts, depth, hidden), f32)
        grad_up = grad_gate
        for shift in range(inner):
            start = (me_i - shift) % inner * own_experts
            gate, up = (
                jnp.swapaxes(part.reshape(depth, own_experts, hidden), 0, 1).astype(f32)
                for part in sent_gate_up[shift]
            )
            grad_gate = put(grad_gate, gate, start, 0, 0)
            grad_up = put(grad_up, up, start, 0, 0)
        return (
            mixed,
            grad_tokens,
            side_sum[n_experts],
            shard_attn[:, :q_cols],
            shard_attn[:, q_cols : q_cols + k_cols],
            shard_attn[:, q_cols + k_cols : qkv_cols],
            shard_attn[:, qkv_cols:attn_cols].T,
            side_sum[n_experts + 1],
            side_sum[:n_experts].T,
            grad_gate,
            grad_up,
            grad_down,
        )

    in_specs = (
        P(("i", "o", "t"), None),
        P(("i", "o", "t"), None),
        P(dp),
        P(dp, None),
        P(dp),
        P(dp, "t"),
        P(dp, "t"),
        P(dp, "t"),
        P("t", dp),
        P(dp),
        P(dp, None),
        P(None, dp, "t"),
        P(None, dp, "t"),
        P(None, "t", dp),
    )
    out_specs = (
        P(("i", "o", "t"), None),
        P(("i", "o", "t"), None),
        P(dp),
        P(dp, "t"),
        P(dp, "t"),
        P(dp, "t"),
        P("t", dp),
        P(dp),
        P(dp, None),
        P(None, dp, "t"),
        P(None, dp, "t"),
        P(None, "t", dp),
    )
    return jax.shard_map(
        on_device, mesh=grid, in_specs=in_specs, out_specs=out_specs, check_vma=False
    )
```
